512 devices in a mesh: samp: 64 (over z, x), blk: 8 (over y, core).
Axes of the slice: x: 4, y: 4, z: 16, core: 2. Of those that a mesh axis runs over, the one named last changes fastest.
Arguments:
- genotypes: bfloat16 [65536, 4000], P('samp', 'blk'), may hold values from 0 to 2, as said below
- traits: float32 [65536, 8], P('samp'), may hold values from -3000 to 3000
- observed: int32 [65536, 8], P('samp'), may hold values from 0 to 1, as said below
- fold_index: int32 [65536], P('samp'), may hold values from 0 to 4, never falling along the last dimension, each value on 1 to 26214 neighbouring positions
Outputs:
- stack_gram: float32 [8, 5, 40, 40], P('blk')
- stack_cross: float32 [8, 5, 40], P('blk')
The draws below stay inside these ranges and needn't reach their ends.
Inputs may be any that keep to these rules, and one draw needn't show every extreme that they name: `genotypes`: genotype dosages, whole numbers. `observed`: each trait is measured in at least one sample.
All inputs are finite; a program needn't handle non-finite values.
Results may differ from the reference program's by a relative error of at most 0.0003.
Values sent between devices are 32-bit elements; how exact they have to be, the bound alone decides.
A program may use at most 64 MiB of HBM per device.

```python
import math
import jax
import jax.numpy as jnp
import numpy as np
from jax import lax

BLOCK = 500
TRAITS = 8
FOLDS = 5
SAMPLES = 65536
BLOCKS = 8
SNPS = 4000


def dosage_draw(key):
    base_key = jax.random.fold_in(key, 11)
    freq_key, allele_key, link_key = jax.random.split(base_key, 3)
    baseline = jax.random.randint(freq_key, (SNPS,), 20, 334)
    row_ids = jnp.arange(SAMPLES, dtype=jnp.int32)
    threshold = baseline[None, :] * (SAMPLES + 2 * row_ids[:, None]) // SAMPLES
    dice_rolls = jax.random.randint(allele_key, (SAMPLES, SNPS), 0, 10000000)
    first_allele = (dice_rolls % 1000 < threshold).astype(jnp.int32)
    second_allele = (dice_rolls // 1000 % 1000 < threshold).astype(jnp.int32)
    fresh = first_allele + second_allele
    link_level = jax.random.randint(link_key, (SNPS,), 5, 10)
    snp_ids = jnp.arange(SNPS, dtype=jnp.int32)
    linked = jnp.logical_and(dice_rolls // 1000000 < link_level[None, :], snp_ids[None, :] > 0)
    run_start = jnp.where(linked, 0, snp_ids[None, :]).astype(jnp.int32)
    source = lax.cummax(run_start, axis=1)
    return jnp.take_along_axis(fresh, source, axis=1)


def draw_genotypes(key, part):
    return dosage_draw(key).astype(jnp.float32).astype(jnp.bfloat16)


def draw_traits(key, part):
    dosage = dosage_draw(key)
    trait_key = jax.random.fold_in(key, 23)
    sub_keys = jax.random.split(trait_key, 5)
    effects = jax.random.randint(sub_keys[0], (SNPS, TRAITS), -1, 2)
    signal = jnp.dot(dosage, effects).astype(jnp.float32)
    genetic = jnp.clip(signal / math.sqrt(0.25 * SNPS), -6.0, 6.0)
    heritability = jax.random.uniform(sub_keys[1], (TRAITS,), minval=0.2, maxval=0.8)
    trait_scale = jnp.exp(jax.random.uniform(sub_keys[2], (TRAITS,), minval=0.0, maxval=math.log(10.0)))
    position = jnp.arange(SAMPLES, dtype=jnp.float32) / (SAMPLES - 1)
    row_scale = jnp.exp(math.log(10.0) * position)[:, None]
    trait_shift = jax.random.uniform(sub_keys[3], (TRAITS,), minval=-3.0, maxval=3.0)
    noise_part = jnp.clip(jax.random.normal(sub_keys[4], (SAMPLES, TRAITS)), -4.0, 4.0)
    mixture = jnp.sqrt(heritability) * genetic + jnp.sqrt(1.0 - heritability) * noise_part
    return (trait_shift + trait_scale * row_scale * mixture).astype(jnp.float32)


def draw_observed(key, part):
    base_key = jax.random.fold_in(key, 37)
    keep_key, roll_key = jax.random.split(base_key)
    keep_level = jax.random.randint(keep_key, (TRAITS,), 5, 10)
    dice_rolls = jax.random.randint(roll_key, (SAMPLES, TRAITS), 0, 10)
    first_row = (jnp.arange(SAMPLES, dtype=jnp.int32) == 0)[:, None]
    measured = (dice_rolls < keep_level[None, :]).astype(jnp.int32)
    return jnp.where(first_row, 1, measured).astype(jnp.int32)


def profile(amount, total, bound, lean):
    portions = [(1 << 20) // math.isqrt(grade ** lean) + 1 for grade in range(2, amount + 1)]
    rest, holding = total - bound - (amount - 1), [1] * (amount - 1)
    while rest > 0:
        movable = [i for i in range(amount - 1) if holding[i] < bound]
        mass, left = sum([portions[i] for i in movable]), rest
        for i in movable:
            extra = min(bound - holding[i], max(1, left * portions[i] // mass), rest)
            holding[i] = holding[i] + extra
            rest = rest - extra
    return np.array([bound] + holding)


def uneven_parts(stream_key, count, total, limit, slope):
    if count == 2:
        one = jax.random.randint(stream_key, (), max(1, total - limit), min(limit, total - 1) + 1)
        return jnp.stack([one, total - one])
    tallies = jnp.asarray(profile(count, total, limit, slope), jnp.int32)
    couples = (count - 1) // 2
    giver, taker = tallies[1:1 + 2 * couples:2], tallies[2:2 + 2 * couples:2]
    room = jnp.minimum(giver - 1, limit - taker)
    moved = jax.random.randint(jax.random.fold_in(stream_key, 1), (couples,), 0, 1 << 20) % (room + 1)
    tallies = tallies.at[1:1 + 2 * couples:2].set(giver - moved).at[2:2 + 2 * couples:2].set(taker + moved)
    return tallies[jax.random.permutation(jax.random.fold_in(stream_key, 2), count)]


def setup_inputs(seed: int = 0) -> dict:
    streams_of = jax.random.split(jax.random.key(seed), 5)
    return {
        "genotypes": draw_genotypes(jax.random.fold_in(streams_of[4], 71), 0),
        "traits": draw_traits(jax.random.fold_in(streams_of[4], 71), 0),
        "observed": draw_observed(jax.random.fold_in(streams_of[4], 71), 0),
        "fold_index": jnp.searchsorted(jnp.cumsum(uneven_parts(streams_of[3], FOLDS, SAMPLES, 2 * SAMPLES // FOLDS, 1)), jnp.arange(SAMPLES), side="right").astype(jnp.int32),
    }


HERITABILITY = (0.01, 0.25, 0.5, 0.75, 0.99)
PRECISE = lax.Precision.HIGHEST

def reference(genotypes, traits, observed, fold_index):
    present = observed.astype(jnp.float32)
    masked = present * traits
    counts = lax.optimization_barrier(jnp.sum(present, 0))
    mean_trait = lax.optimization_barrier(jnp.sum(masked, 0)) / counts
    trait_scale = jnp.sqrt(lax.optimization_barrier(jnp.sum(masked * traits, 0)) / counts - mean_trait * mean_trait + 1e-05)
    scaled = present * (traits - mean_trait) / trait_scale
    identity = jnp.eye(BLOCK, dtype=jnp.float32)
    columns = []
    for block_index in range(BLOCKS):
        dosage = genotypes[:, block_index * BLOCK:(block_index + 1) * BLOCK].astype(jnp.float32)
        gram_block = jnp.dot(dosage.T, dosage, precision=PRECISE)
        column_sums = lax.optimization_barrier(jnp.sum(dosage, 0))
        mean_dosage = column_sums / SAMPLES
        dosage_scale = jnp.sqrt(jnp.diagonal(gram_block) / SAMPLES - mean_dosage * mean_dosage + 1e-05)
        covariance = (gram_block - column_sums[:, None] * column_sums[None, :] / SAMPLES) / (dosage_scale[:, None] * dosage_scale[None, :])
        dosage_trait = jnp.dot(dosage.T, masked, precision=PRECISE)
        dosage_present = jnp.dot(dosage.T, present, precision=PRECISE)
        right_side = (dosage_trait - dosage_present * mean_trait) / trait_scale / dosage_scale[:, None]
        centred = (dosage - mean_dosage) / dosage_scale
        for fraction in HERITABILITY:
            lower_factor = jnp.linalg.cholesky(covariance + SNPS * (1.0 - fraction) / fraction * identity)
            solution = jax.scipy.linalg.cho_solve((lower_factor, True), right_side)
            predicted = jnp.dot(centred, solution, precision=PRECISE)
            energy = lax.optimization_barrier(jnp.sum(predicted * predicted, 0))
            columns.append(predicted / jnp.sqrt(energy / SAMPLES + 1e-06))
    standard = jnp.stack(columns, 2)
    fold_hits = (fold_index[None, :] == jnp.arange(FOLDS, dtype=jnp.int32)[:, None]).astype(jnp.float32)
    gram_list = []
    cross_list = []
    for trait_index in range(TRAITS):
        stacked = standard[:, trait_index, :]
        weighting = fold_hits * present[:, trait_index][None, :]
        weighted = weighting[:, :, None] * stacked[None]
        gram_sum = jnp.einsum('ksl,sm->klm', weighted, stacked, precision=PRECISE)
        cross_sum = jnp.einsum('ksl,s->kl', weighted, scaled[:, trait_index], precision=PRECISE)
        gram_list.append(gram_sum * (FOLDS / SAMPLES))
        cross_list.append(cross_sum * (FOLDS / SAMPLES))
    return (jnp.stack(gram_list, 0), jnp.stack(cross_list, 0))
```

```python
import functools

import jax
import jax.numpy as jnp
from jax import lax
from jax.experimental import pallas as pl
from jax.experimental.pallas import tpu as pltpu
from jax.sharding import PartitionSpec as P

BLOCK = 500
TRAITS = 8
FOLDS = 5
HERITABILITY = (0.01, 0.25, 0.5, 0.75, 0.99)
PENALTIES = len(HERITABILITY)
PRECISE = lax.Precision.HIGHEST
MESH = pl.DeviceIdType.MESH

XS = 4
LANES = 128
TILES = 4
WIDTH = TILES * LANES
ONES = BLOCK
PAIRS = [(i, j) for i in range(TILES) for j in range(i, TILES)]
EXTRA = 24
FLAT = len(PAIRS) * LANES + TILES * EXTRA
QUARTER = FLAT // XS
HALF = 176
STACK = PENALTIES * 8


def pieces(start, rows):
    out = []
    while rows > 0:
        quarter, row = divmod(start, QUARTER)
        take = min(rows, QUARTER - row)
        out.append((quarter, row, take))
        start += take
        rows -= take
    return out


def put(ref, start, value):
    done = 0
    for quarter, row, take in pieces(start, value.shape[0]):
        ref[quarter, row : row + take, :] = value[done : done + take]
        done += take


def get(ref, start, rows):
    parts = [ref[quarter, row : row + take, :] for quarter, row, take in pieces(start, rows)]
    return parts[0] if len(parts) == 1 else jnp.concatenate(parts, axis=0)


def split3(value):
    first = value.astype(jnp.bfloat16).astype(jnp.float32)
    rest = value - first
    second = rest.astype(jnp.bfloat16).astype(jnp.float32)
    third = rest - second
    return first, second, third


def remote(src, dst, send, recv, samp, blk):
    return pltpu.make_async_remote_copy(
        src_ref=src,
        dst_ref=dst,
        send_sem=send,
        recv_sem=recv,
        device_id=(samp, blk),
        device_id_type=MESH,
    )


def gram_kernel(
    zs, chunk, g_ref, aux_ref, out_ref, g_scr, pay, from_left, from_right, acc, z_in, mine, z_all,
    total, xs_send, xs_recv, zr_send, zr_recv, zg_send, zg_recv, xg_send, xg_recv,
):
    samp = lax.axis_index("samp")
    blk = lax.axis_index("blk")
    z = samp // XS
    x = lax.rem(samp, XS)
    right = lax.rem(x + 1, XS)
    left = lax.rem(x + XS - 1, XS)
    far = lax.rem(x + 2, XS)
    to_right = z * XS + right
    to_left = z * XS + left

    barrier = pltpu.get_barrier_semaphore()
    for side in (to_right, to_left):
        pl.semaphore_signal(barrier, inc=1, device_id=(side, blk), device_id_type=MESH)

    def greet(i, carry):
        other = lax.rem(z + i + 1, zs) * XS + x
        pl.semaphore_signal(barrier, inc=1, device_id=(other, blk), device_id_type=MESH)
        return carry

    lax.fori_loop(0, zs - 1, greet, 0)

    rows = g_ref.shape[0]
    tail = lax.broadcasted_iota(jnp.int32, (rows, LANES), 1) == ONES - (TILES - 1) * LANES
    g_scr[:, (TILES - 1) * LANES :] = tail.astype(jnp.float32).astype(jnp.bfloat16)
    g_scr[:, :BLOCK] = g_ref[...]
    traits = aux_ref[0:8, :]
    present = aux_ref[8:16, :]
    masked = traits * present
    squares = jnp.sum(masked * traits, axis=1, keepdims=True)
    ones = (lax.broadcasted_iota(jnp.int32, masked.shape, 0) == 0).astype(jnp.float32)
    stacked = jnp.concatenate([*split3(masked), present, ones], axis=0).astype(jnp.bfloat16)
    products = jnp.dot(stacked, g_scr[...], preferred_element_type=jnp.float32)
    for j in range(TILES):
        cols = products[:, j * LANES : (j + 1) * LANES]
        last = cols[32:40]
        if j == TILES - 1:
            lane = lax.broadcasted_iota(jnp.int32, last.shape, 1)
            last = jnp.where(lane == ONES + 1 - j * LANES, squares, last)
        base = len(PAIRS) * LANES + j * EXTRA
        put(pay, base, cols[0:8] + (cols[8:16] + cols[16:24]))
        put(pay, base + 8, cols[24:32])
        put(pay, base + 16, last)
    slot = 0
    for i in range(TILES):
        strip = lax.dot_general(
            g_scr[:, i * LANES : (i + 1) * LANES],
            g_scr[:, i * LANES :],
            (((0,), (0,)), ((), ())),
            preferred_element_type=jnp.float32,
        )
        for j in range(i, TILES):
            put(pay, slot * LANES, strip[:, (j - i) * LANES : (j - i + 1) * LANES])
            slot += 1
    acc[QUARTER:, :] = jnp.zeros((acc.shape[0] - QUARTER, LANES), jnp.float32)

    pl.semaphore_wait(barrier, 2 + zs - 1)

    first = pl.ds(0, HALF)
    second = pl.ds(HALF, QUARTER - HALF)
    a1 = remote(pay.at[far, first], from_left.at[0, first], xs_send.at[0], xs_recv.at[0], to_right, blk)
    a2 = remote(pay.at[far, second], from_right.at[0, second], xs_send.at[1], xs_recv.at[1], to_left, blk)
    a3 = remote(pay.at[right, second], from_left.at[1, second], xs_send.at[2], xs_recv.at[2], to_right, blk)
    a4 = remote(pay.at[left, first], from_right.at[1, first], xs_send.at[3], xs_recv.at[3], to_left, blk)
    a5 = remote(pay.at[right, first], from_left.at[1, first], xs_send.at[4], xs_recv.at[4], to_right, blk)
    a6 = remote(pay.at[left, second], from_right.at[1, second], xs_send.at[5], xs_recv.at[5], to_left, blk)
    a1.start()
    a2.start()
    a3.start()
    a4.start()
    a1.wait_recv()
    pay[right, 0:HALF, :] = pay[right, 0:HALF, :] + from_left[0, 0:HALF, :]
    a5.start()
    a2.wait_recv()
    pay[left, HALF:QUARTER, :] = pay[left, HALF:QUARTER, :] + from_right[0, HALF:QUARTER, :]
    a6.start()
    for copy in (a3, a4, a5, a6):
        copy.wait_recv()
    acc[0:QUARTER, :] = pay[x, 0:QUARTER, :] + (from_left[1, 0:QUARTER, :] + from_right[1, 0:QUARTER, :])

    def scatter(i):
        other = lax.rem(z + i + 1, zs)
        rows_there = pl.ds(pl.multiple_of(other * chunk, 8), chunk)
        return remote(acc.at[rows_there], z_in.at[i], zr_send.at[i], zr_recv.at[i], other * XS + x, blk)

    def start_scatter(i, carry):
        scatter(i).start()
        return carry

    def wait_scatter(i, carry):
        scatter(i).wait_recv()
        return carry

    lax.fori_loop(0, zs - 1, start_scatter, 0)
    lax.fori_loop(0, zs - 1, wait_scatter, 0)
    here = acc[pl.ds(pl.multiple_of(z * chunk, 8), chunk), :]
    for i in range(zs - 1):
        here = here + z_in[i]
    mine[...] = here
    mine_rows = pl.ds(pl.multiple_of(z * chunk, 8), chunk)
    z_all[mine_rows, :] = here

    def gather(i):
        other = lax.rem(z + i + 1, zs)
        return remote(mine, z_all.at[mine_rows], zg_send.at[i], zg_recv.at[i], other * XS + x, blk)

    def start_gather(i, carry):
        gather(i).start()
        return carry

    def wait_gather(i, carry):
        gather(i).wait_recv()
        return carry

    lax.fori_loop(0, zs - 1, start_gather, 0)
    lax.fori_loop(0, zs - 1, wait_gather, 0)

    quarter = pl.ds(0, QUARTER)
    b1 = remote(z_all.at[quarter], total.at[x, quarter], xg_send.at[0], xg_recv.at[0], to_right, blk)
    b2 = remote(z_all.at[quarter], total.at[x, quarter], xg_send.at[1], xg_recv.at[1], to_left, blk)
    b3 = remote(total.at[left, first], total.at[left, first], xg_send.at[2], xg_recv.at[2], to_right, blk)
    b4 = remote(total.at[right, second], total.at[right, second], xg_send.at[3], xg_recv.at[3], to_left, blk)
    b1.start()
    b2.start()
    total[x, 0:QUARTER, :] = z_all[0:QUARTER, :]
    b1.wait_recv()
    b3.start()
    b2.wait_recv()
    b4.start()
    b3.wait_recv()
    b4.wait_recv()
    out_ref[...] = total[...]

    for copy in (a1, a2, a3, a4, a5, a6, b1, b2, b3, b4):
        copy.wait_send()

    def drain(i, carry):
        scatter(i).wait_send()
        gather(i).wait_send()
        return carry

    lax.fori_loop(0, zs - 1, drain, 0)


def sum_grams(genotypes, aux, zs):
    chunk = -(-QUARTER // (8 * zs)) * 8
    rows = genotypes.shape[0]
    vmem = pl.BlockSpec(memory_space=pltpu.VMEM)
    dma = pltpu.SemaphoreType.DMA
    return pl.pallas_call(
        functools.partial(gram_kernel, zs, chunk),
        out_shape=jax.ShapeDtypeStruct((XS, QUARTER, LANES), jnp.float32),
        in_specs=[vmem, vmem],
        out_specs=vmem,
        scratch_shapes=[
            pltpu.VMEM((rows, WIDTH), jnp.bfloat16),
            pltpu.VMEM((XS, QUARTER, LANES), jnp.float32),
            pltpu.VMEM((2, QUARTER, LANES), jnp.float32),
            pltpu.VMEM((2, QUARTER, LANES), jnp.float32),
            pltpu.VMEM((zs * chunk, LANES), jnp.float32),
            pltpu.VMEM((zs - 1, chunk, LANES), jnp.float32),
            pltpu.VMEM((chunk, LANES), jnp.float32),
            pltpu.VMEM((zs * chunk, LANES), jnp.float32),
            pltpu.VMEM((XS, QUARTER, LANES), jnp.float32),
            dma((6,)),
            dma((6,)),
            dma((zs - 1,)),
            dma((zs - 1,)),
            dma((zs - 1,)),
            dma((zs - 1,)),
            dma((4,)),
            dma((4,)),
        ],
        compiler_params=pltpu.CompilerParams(
            collective_id=0, has_side_effects=True, vmem_limit_bytes=48 << 20
        ),
        name="sum_grams",
    )(genotypes, aux)


def invert(a_ref):
    lane = lax.broadcasted_iota(jnp.int32, (8, LANES), 1)
    sub = lax.broadcasted_iota(jnp.int32, (8, LANES), 0)
    wide = lax.broadcasted_iota(jnp.int32, (LANES, LANES), 1)

    def panel(q, carry):
        base = pl.multiple_of(q * 8, 8)
        shift = lax.rem(LANES - base, LANES)
        strip = a_ref[pl.ds(base, 8), :]
        turned = pltpu.roll(strip, shift, 1)
        cols = [jnp.broadcast_to(turned[:, j : j + 1], (8, LANES)) for j in range(8)]
        inside = jnp.logical_and(lane >= base, lane < base + 8)
        solved = jnp.where(inside, jnp.where(lane - base == sub, -1.0, 0.0), strip)
        for j in range(8):
            inverse = 1.0 / cols[j][j : j + 1, :]
            row = solved[j : j + 1, :] * inverse
            solved = jnp.where(sub == j, row, solved - cols[j] * row)
            for m in range(j + 1, 8):
                value = cols[m][j : j + 1, :] * inverse
                cols[m] = jnp.where(sub == j, value, cols[m] - cols[j] * value)
        whole = a_ref[...]
        turned_all = pltpu.roll(whole, shift, 1)
        within = jnp.logical_and(wide >= base, wide < base + 8)
        result = jnp.where(within, 0.0, whole)
        for j in range(8):
            result = result - turned_all[:, j : j + 1] * solved[j : j + 1, :]
        a_ref[...] = result
        a_ref[pl.ds(base, 8), :] = solved
        return carry

    lax.fori_loop(0, LANES // 8, panel, 0)


def solve_kernel(samples, markers, total_ref, beta_ref, stat_ref, cov, work, inv):
    samp = lax.axis_index("samp")
    place = lax.rem(samp, 2 * XS)
    weight = jnp.float32(0.0)
    for r, fraction in enumerate(HERITABILITY):
        value = jnp.float32(markers * (1.0 - fraction) / fraction)
        chosen = place == r if r < PENALTIES - 1 else place >= r
        weight = jnp.where(chosen, value, weight)

    dot = functools.partial(jnp.dot, precision=PRECISE, preferred_element_type=jnp.float32)

    def dot_t(a, b):
        return lax.dot_general(
            a, b, (((0,), (0,)), ((), ())), precision=PRECISE, preferred_element_type=jnp.float32
        )

    def dot_nt(a, b):
        return lax.dot_general(
            a, b, (((1,), (1,)), ((), ())), precision=PRECISE, preferred_element_type=jnp.float32
        )

    slot = {pair: n for n, pair in enumerate(PAIRS)}
    gram = {pair: get(total_ref, n * LANES, LANES) for pair, n in slot.items()}
    extra = [get(total_ref, len(PAIRS) * LANES + j * EXTRA, EXTRA) for j in range(TILES)]
    eye = lax.broadcasted_iota(jnp.int32, (LANES, LANES), 0) == lax.broadcasted_iota(
        jnp.int32, (LANES, LANES), 1
    )
    mark = ONES - (TILES - 1) * LANES
    sums = extra[-1][0:8, mark : mark + 1]
    counts = extra[-1][8:16, mark : mark + 1]
    squares = extra[-1][16:24, mark + 1 : mark + 2]
    mean_trait = sums / counts
    trait_scale = jnp.sqrt(squares / counts - mean_trait * mean_trait + 1e-05)
    lane8 = lax.broadcasted_iota(jnp.int32, (8, LANES), 1)
    stat_ref[...] = jnp.where(lane8 == 0, mean_trait, jnp.where(lane8 == 1, trait_scale, 0.0))

    sum_row, mean_row, scale_row, sum_col, scale_col = [], [], [], [], []
    for j in range(TILES):
        diagonal = jnp.where(eye, gram[(j, j)], 0.0)
        row = extra[j][16:17, :]
        if j == TILES - 1:
            row = jnp.where(lane8[0:1] < mark, row, 0.0)
        col = gram[(j, TILES - 1)][:, mark : mark + 1]
        mean = row / samples
        mean_c = col / samples
        sum_row.append(row)
        mean_row.append(mean)
        sum_col.append(col)
        squares_row = jnp.sum(diagonal, axis=0, keepdims=True)
        squares_col = jnp.sum(diagonal, axis=1, keepdims=True)
        scale_row.append(jnp.sqrt(squares_row / samples - mean * mean + 1e-05))
        scale_col.append(jnp.sqrt(squares_col / samples - mean_c * mean_c + 1e-05))
    lane = lax.broadcasted_iota(jnp.int32, (LANES, LANES), 1)
    sub = lax.broadcasted_iota(jnp.int32, (LANES, LANES), 0)
    for (i, j), n in slot.items():
        value = (gram[(i, j)] - sum_col[i] * sum_row[j] / samples) / (scale_col[i] * scale_row[j])
        if j == TILES - 1:
            value = jnp.where(lane < mark, value, 0.0)
        if i == TILES - 1:
            value = jnp.where(sub < mark, value, 0.0)
        cov[n] = value
        work[n] = jnp.where(eye, value + weight, value) if i == j else value
    side = []
    for j in range(TILES):
        value = (extra[j][0:8] - extra[j][8:16] * mean_trait) / trait_scale / scale_row[j]
        if j == TILES - 1:
            value = jnp.where(lane8 < mark, value, 0.0)
        side.append(value)

    for k in range(TILES):
        a_ref = inv.at[k]
        a_ref[...] = work[slot[(k, k)]]
        invert(a_ref)
        minus = inv[k]
        for j in range(k + 1, TILES):
            ahead = dot(minus, work[slot[(k, j)]])
            for i in range(k + 1, j + 1):
                n = slot[(i, j)]
                work[n] = work[n] + dot_t(work[slot[(k, i)]], ahead)
        if k < TILES - 1:
            part = dot(side[k], minus)
            for j in range(k + 1, TILES):
                side[j] = side[j] + dot(part, work[slot[(k, j)]])

    found = [None] * TILES
    for k in range(TILES - 1, -1, -1):
        value = side[k]
        for j in range(k + 1, TILES):
            value = value - dot_nt(found[j], work[slot[(k, j)]])
        found[k] = -dot(value, inv[k])

    energy = jnp.zeros((8, 1), jnp.float32)
    shift = jnp.zeros((8, 1), jnp.float32)
    betas = []
    for k in range(TILES):
        image = dot(found[k], cov[slot[(k, k)]])
        for j in range(k + 1, TILES):
            image = image + 2.0 * dot_nt(found[j], cov[slot[(k, j)]])
        energy = energy + jnp.sum(image * found[k], axis=1, keepdims=True)
        beta = found[k] / scale_row[k]
        shift = shift + jnp.sum(beta * mean_row[k], axis=1, keepdims=True)
        betas.append(beta)
    norm = 1.0 / jnp.sqrt(energy / samples + 1e-06)
    for k in range(TILES):
        value = betas[k]
        if k == TILES - 1:
            value = jnp.where(lane8 == mark, -shift, jnp.where(lane8 < mark, value, 0.0))
        beta_ref[:, k * LANES : (k + 1) * LANES] = value * norm


def solve(total, samples, markers):
    vmem = pl.BlockSpec(memory_space=pltpu.VMEM)
    return pl.pallas_call(
        functools.partial(solve_kernel, samples, markers),
        out_shape=(
            jax.ShapeDtypeStruct((8, WIDTH), jnp.float32),
            jax.ShapeDtypeStruct((8, LANES), jnp.float32),
        ),
        in_specs=[vmem],
        out_specs=(vmem, vmem),
        scratch_shapes=[
            pltpu.VMEM((len(PAIRS), LANES, LANES), jnp.float32),
            pltpu.VMEM((len(PAIRS), LANES, LANES), jnp.float32),
            pltpu.VMEM((TILES, LANES, LANES), jnp.float32),
        ],
        compiler_params=pltpu.CompilerParams(vmem_limit_bytes=48 << 20),
        name="solve",
    )(total)


def share_kernel(beta_ref, out_ref, held, send, recv):
    samp = lax.axis_index("samp")
    blk = lax.axis_index("blk")
    group = 2 * XS
    place = lax.rem(samp, group)
    first = samp - place
    barrier = pltpu.get_barrier_semaphore()
    for i in range(group - 1):
        other = first + lax.rem(place + i + 1, group)
        pl.semaphore_signal(barrier, inc=1, device_id=(other, blk), device_id_type=MESH)
    pl.semaphore_wait(barrier, group - 1)

    def copy(i):
        other = first + lax.rem(place + i + 1, group)
        return remote(beta_ref, held.at[place], send.at[i], recv.at[place], other, blk)

    @pl.when(place < PENALTIES)
    def _():
        for i in range(group - 1):
            copy(i).start()
        held[place] = beta_ref[...]

    for r in range(PENALTIES):

        @pl.when(place != r)
        def _():
            pltpu.make_async_copy(held.at[r], held.at[r], recv.at[r]).wait()

    out_ref[...] = jnp.zeros_like(out_ref)
    for r in range(PENALTIES):
        out_ref[:, r, :] = held[r]

    @pl.when(place < PENALTIES)
    def _():
        for i in range(group - 1):
            copy(i).wait_send()


def share(beta):
    vmem = pl.BlockSpec(memory_space=pltpu.VMEM)
    return pl.pallas_call(
        share_kernel,
        out_shape=jax.ShapeDtypeStruct((TRAITS, 8, WIDTH), jnp.float32),
        in_specs=[vmem],
        out_specs=vmem,
        scratch_shapes=[
            pltpu.VMEM((PENALTIES, 8, WIDTH), jnp.float32),
            pltpu.SemaphoreType.DMA((2 * XS - 1,)),
            pltpu.SemaphoreType.DMA((PENALTIES,)),
        ],
        compiler_params=pltpu.CompilerParams(collective_id=1, has_side_effects=True),
        name="share",
    )(beta)


PARTS = 24


def stack_kernel(
    zs, factor, g_ref, aux_ref, beta_ref, stat_ref, out_ref, g_scr, outgoing, incoming, columns,
    weights, part, x_in, z_all, mine, total, a_send, a_recv, xs_send, xs_recv, z_send, z_recv,
    xg_send, xg_recv,
):
    samp = lax.axis_index("samp")
    blk = lax.axis_index("blk")
    z = samp // XS
    x = lax.rem(samp, XS)
    barrier = pltpu.get_barrier_semaphore()

    def trait_peer(i):
        return lax.rem(blk + i + 1, TRAITS)

    def x_peer(i):
        return z * XS + lax.rem(x + i + 1, XS)

    def z_peer(i):
        return lax.rem(z + i + 1, zs) * XS + x

    for i in range(TRAITS - 1):
        pl.semaphore_signal(barrier, inc=1, device_id=(samp, trait_peer(i)), device_id_type=MESH)
    for i in range(XS - 1):
        pl.semaphore_signal(barrier, inc=1, device_id=(x_peer(i), blk), device_id_type=MESH)

    def greet(i, carry):
        pl.semaphore_signal(barrier, inc=1, device_id=(z_peer(i), blk), device_id_type=MESH)
        return carry

    lax.fori_loop(0, zs - 1, greet, 0)

    rows = g_ref.shape[0]
    tail = lax.broadcasted_iota(jnp.int32, (rows, LANES), 1) == ONES - (TILES - 1) * LANES
    g_scr[:, (TILES - 1) * LANES :] = tail.astype(jnp.float32).astype(jnp.bfloat16)
    g_scr[:, :BLOCK] = g_ref[...]
    beta = beta_ref[...].reshape(TRAITS * 8, WIDTH)
    stacked = jnp.concatenate(split3(beta), axis=0).astype(jnp.bfloat16)
    predicted = lax.dot_general(
        stacked, g_scr[...], (((1,), (1,)), ((), ())), preferred_element_type=jnp.float32
    )
    n = TRAITS * 8
    predicted = predicted[0:n] + (predicted[n : 2 * n] + predicted[2 * n :])
    outgoing[...] = predicted.reshape(TRAITS, 8, rows)

    which = lax.broadcasted_iota(jnp.int32, (8, rows), 0) == blk
    present = jnp.sum(jnp.where(which, aux_ref[8:16, :], 0.0), axis=0, keepdims=True)
    mean = stat_ref[:, 0:1]
    scale = stat_ref[:, 1:2]
    scaled_all = aux_ref[8:16, :] * (aux_ref[0:8, :] - mean) / scale
    scaled = jnp.sum(jnp.where(which, scaled_all, 0.0), axis=0, keepdims=True)
    fold = aux_ref[16:17, :]

    pl.semaphore_wait(barrier, TRAITS - 1 + XS - 1 + zs - 1)

    def exchange(i):
        other = trait_peer(i)
        return remote(outgoing.at[other], incoming.at[blk], a_send.at[i], a_recv.at[i], samp, other)

    for i in range(TRAITS - 1):
        exchange(i).start()
    incoming[blk] = outgoing[blk]
    for i in range(TRAITS - 1):
        exchange(i).wait_recv()

    for b in range(TRAITS):
        columns[b * PENALTIES : (b + 1) * PENALTIES, :] = incoming[b, 0:PENALTIES, :]
    stacked_cols = columns[...]
    for k in range(FOLDS):
        hit = jnp.where(fold == float(k), present, 0.0)
        weights[k * STACK : (k + 1) * STACK, :] = stacked_cols * hit
    end = FOLDS * STACK
    picked = lax.broadcasted_iota(jnp.int32, (8, rows), 0).astype(jnp.float32) == fold
    weights[end : end + 8, :] = jnp.where(picked, scaled, 0.0)
    weights[end + 8 :, :] = jnp.zeros((weights.shape[0] - end - 8, rows), jnp.float32)
    local = lax.dot_general(
        stacked_cols,
        weights[...],
        (((1,), (1,)), ((), ())),
        precision=PRECISE,
        preferred_element_type=jnp.float32,
    )
    flat = jnp.concatenate(
        [
            local[:, 0:LANES],
            local[:, LANES:],
            jnp.zeros((XS * PARTS - 2 * STACK, LANES), jnp.float32),
        ],
        axis=0,
    )
    for q in range(XS):
        part[q] = flat[q * PARTS : (q + 1) * PARTS]

    def scatter(i):
        there = lax.rem(x + i + 1, XS)
        return remote(part.at[there], x_in.at[i], xs_send.at[i], xs_recv.at[i], x_peer(i), blk)

    for i in range(XS - 1):
        scatter(i).start()
    for i in range(XS - 1):
        scatter(i).wait_recv()
    value = part[x] + (x_in[0] + (x_in[1] + x_in[2]))
    mine[...] = value
    z_all[z] = value

    def spread(i):
        return remote(mine, z_all.at[z], z_send.at[i], z_recv.at[i], z_peer(i), blk)

    def start_spread(i, carry):
        spread(i).start()
        return carry

    def wait_spread(i, carry):
        spread(i).wait_recv()
        return carry

    lax.fori_loop(0, zs - 1, start_spread, 0)
    lax.fori_loop(0, zs - 1, wait_spread, 0)
    value = z_all[0]
    for i in range(1, zs):
        value = value + z_all[i]
    total[x] = value * factor

    def collect(i):
        return remote(total.at[x], total.at[x], xg_send.at[i], xg_recv.at[i], x_peer(i), blk)

    for i in range(XS - 1):
        collect(i).start()
    for i in range(XS - 1):
        collect(i).wait_recv()
    out_ref[...] = total[...]

    for i in range(TRAITS - 1):
        exchange(i).wait_send()
    for i in range(XS - 1):
        scatter(i).wait_send()
        collect(i).wait_send()

    def drain(i, carry):
        spread(i).wait_send()
        return carry

    lax.fori_loop(0, zs - 1, drain, 0)


def stack(genotypes, aux, betas, stats, zs, factor):
    rows = genotypes.shape[0]
    vmem = pl.BlockSpec(memory_space=pltpu.VMEM)
    dma = pltpu.SemaphoreType.DMA
    return pl.pallas_call(
        functools.partial(stack_kernel, zs, factor),
        out_shape=jax.ShapeDtypeStruct((XS, PARTS, LANES), jnp.float32),
        in_specs=[vmem] * 4,
        out_specs=vmem,
        scratch_shapes=[
            pltpu.VMEM((rows, WIDTH), jnp.bfloat16),
            pltpu.VMEM((TRAITS, 8, rows), jnp.float32),
            pltpu.VMEM((TRAITS, 8, rows), jnp.float32),
            pltpu.VMEM((STACK, rows), jnp.float32),
            pltpu.VMEM((2 * LANES, rows), jnp.float32),
            pltpu.VMEM((XS, PARTS, LANES), jnp.float32),
            pltpu.VMEM((XS - 1, PARTS, LANES), jnp.float32),
            pltpu.VMEM((zs, PARTS, LANES), jnp.float32),
            pltpu.VMEM((PARTS, LANES), jnp.float32),
            pltpu.VMEM((XS, PARTS, LANES), jnp.float32),
            dma((TRAITS - 1,)),
            dma((TRAITS - 1,)),
            dma((XS - 1,)),
            dma((XS - 1,)),
            dma((zs - 1,)),
            dma((zs - 1,)),
            dma((XS - 1,)),
            dma((XS - 1,)),
        ],
        compiler_params=pltpu.CompilerParams(
            collective_id=2, has_side_effects=True, vmem_limit_bytes=48 << 20
        ),
        name="stack",
    )(genotypes, aux, betas, stats)


def body(genotypes, traits, observed, fold_index):
    local_rows, local_cols = genotypes.shape
    sample_devices = lax.axis_size("samp")
    samples = local_rows * sample_devices
    markers = local_cols * lax.axis_size("blk")
    zs = sample_devices // XS
    aux = jnp.concatenate(
        [
            traits.T,
            observed.T.astype(jnp.float32),
            jnp.broadcast_to(fold_index.astype(jnp.float32)[None], (8, local_rows)),
        ],
        axis=0,
    )
    total = sum_grams(genotypes, aux, zs)
    beta, stats = solve(total, samples, markers)
    betas = share(beta)
    flat = stack(genotypes, aux, betas, stats, zs, FOLDS / samples)
    flat = flat.reshape(XS * PARTS, LANES)
    both = jnp.concatenate([flat[0:STACK], flat[STACK : 2 * STACK]], axis=1)
    end = FOLDS * STACK
    grams = both[:, :end].reshape(STACK, FOLDS, STACK).transpose(1, 2, 0)
    cross = both[:, end : end + FOLDS].T
    return grams[None], cross[None]


def solution(mesh):
    in_specs = (P("samp", "blk"), P("samp", None), P("samp", None), P("samp"))
    out_specs = (P("blk", None, None, None), P("blk", None, None))
    return jax.shard_map(body, mesh=mesh, in_specs=in_specs, out_specs=out_specs, check_vma=False)
```

```python
import functools

import jax
import jax.numpy as jnp
from jax import lax
from jax.experimental import pallas as pl
from jax.experimental.pallas import tpu as pltpu
from jax.sharding import PartitionSpec as P

BLOCK = 500
TRAITS = 8
FOLDS = 5
HERITABILITY = (0.01, 0.25, 0.5, 0.75, 0.99)
PENALTIES = len(HERITABILITY)
PRECISE = lax.Precision.HIGHEST
MESH = pl.DeviceIdType.MESH

XS = 4
LANES = 128
TILES = 4
WIDTH = TILES * LANES
ONES = BLOCK
PAIRS = [(i, j) for i in range(TILES) for j in range(i, TILES)]
EXTRA = 24
FLAT = len(PAIRS) * LANES + TILES * EXTRA
QUARTER = FLAT // XS
ZS = 16
CHUNK = 24
LAYERS = ZS * CHUNK
STACK = PENALTIES * 8
SUMS = 48
PARTS = 2 * SUMS // XS
ORDER = [8, 7, 6, 5, -7, -6, -5, -4, 4, 3, 2, 1, -3, -2, -1, 0]
NEAR = [4, -4, 3, -3, 2, -2, 1, -1]
ARRIVAL = [0, -4, 4, -1, 1, -2, 2, -3, 3, -5, 5, -6, 6, -7, 7, -8]
LAG = 3


def pieces(start, rows):
    out = []
    while rows > 0:
        quarter, row = divmod(start, QUARTER)
        take = min(rows, QUARTER - row)
        out.append((quarter, row, take))
        start += take
        rows -= take
    return out


def put(ref, start, value):
    done = 0
    for quarter, row, take in pieces(start, value.shape[0]):
        ref[quarter, row : row + take, :] = value[done : done + take]
        done += take


def get(ref, start, rows):
    parts = [ref[quarter, row : row + take, :] for quarter, row, take in pieces(start, rows)]
    return parts[0] if len(parts) == 1 else jnp.concatenate(parts, axis=0)


def split3(value):
    first = value.astype(jnp.bfloat16).astype(jnp.float32)
    rest = value - first
    second = rest.astype(jnp.bfloat16).astype(jnp.float32)
    third = rest - second
    return first, second, third


def remote(src, dst, send, recv, samp, blk):
    return pltpu.make_async_remote_copy(
        src_ref=src,
        dst_ref=dst,
        send_sem=send,
        recv_sem=recv,
        device_id=(samp, blk),
        device_id_type=MESH,
    )


def invert(a_ref):
    lane = lax.broadcasted_iota(jnp.int32, (8, LANES), 1)
    sub = lax.broadcasted_iota(jnp.int32, (8, LANES), 0)
    wide = lax.broadcasted_iota(jnp.int32, (LANES, LANES), 1)

    def panel(q, carry):
        base = pl.multiple_of(q * 8, 8)
        shift = lax.rem(LANES - base, LANES)
        strip = a_ref[pl.ds(base, 8), :]
        turned = pltpu.roll(strip, shift, 1)
        cols = [jnp.broadcast_to(turned[:, j : j + 1], (8, LANES)) for j in range(8)]
        inside = jnp.logical_and(lane >= base, lane < base + 8)
        solved = jnp.where(inside, jnp.where(lane - base == sub, -1.0, 0.0), strip)
        for j in range(8):
            inverse = 1.0 / cols[j][j : j + 1, :]
            row = solved[j : j + 1, :] * inverse
            solved = jnp.where(sub == j, row, solved - cols[j] * row)
            for m in range(j + 1, 8):
                value = cols[m][j : j + 1, :] * inverse
                cols[m] = jnp.where(sub == j, value, cols[m] - cols[j] * value)
        whole = a_ref[...]
        turned_all = pltpu.roll(whole, shift, 1)
        within = jnp.logical_and(wide >= base, wide < base + 8)
        result = jnp.where(within, 0.0, whole)
        for j in range(8):
            result = result - turned_all[:, j : j + 1] * solved[j : j + 1, :]
        a_ref[...] = result
        a_ref[pl.ds(base, 8), :] = solved
        return carry

    lax.fori_loop(0, LANES // 8, panel, 0)


def solve_local(samples, markers, place, total_ref, beta_ref, stat_ref, cov, work, inv):
    weight = jnp.float32(0.0)
    for r, fraction in enumerate(HERITABILITY):
        value = jnp.float32(markers * (1.0 - fraction) / fraction)
        chosen = place == r if r < PENALTIES - 1 else place >= r
        weight = jnp.where(chosen, value, weight)

    dot = functools.partial(jnp.dot, precision=PRECISE, preferred_element_type=jnp.float32)

    def dot_t(a, b):
        return lax.dot_general(
            a, b, (((0,), (0,)), ((), ())), precision=PRECISE, preferred_element_type=jnp.float32
        )

    def dot_nt(a, b):
        return lax.dot_general(
            a, b, (((1,), (1,)), ((), ())), precision=PRECISE, preferred_element_type=jnp.float32
        )

    slot = {pair: n for n, pair in enumerate(PAIRS)}
    gram = {pair: get(total_ref, n * LANES, LANES) for pair, n in slot.items()}
    extra = [get(total_ref, len(PAIRS) * LANES + j * EXTRA, EXTRA) for j in range(TILES)]
    eye = lax.broadcasted_iota(jnp.int32, (LANES, LANES), 0) == lax.broadcasted_iota(
        jnp.int32, (LANES, LANES), 1
    )
    mark = ONES - (TILES - 1) * LANES
    sums = extra[-1][0:8, mark : mark + 1]
    counts = extra[-1][8:16, mark : mark + 1]
    squares = extra[-1][16:24, mark + 1 : mark + 2]
    mean_trait = sums / counts
    trait_scale = jnp.sqrt(squares / counts - mean_trait * mean_trait + 1e-05)
    lane8 = lax.broadcasted_iota(jnp.int32, (8, LANES), 1)
    stat_ref[...] = jnp.where(lane8 == 0, mean_trait, jnp.where(lane8 == 1, trait_scale, 0.0))

    sum_row, mean_row, scale_row, sum_col, scale_col = [], [], [], [], []
    for j in range(TILES):
        diagonal = jnp.where(eye, gram[(j, j)], 0.0)
        row = extra[j][16:17, :]
        if j == TILES - 1:
            row = jnp.where(lane8[0:1] < mark, row, 0.0)
        col = gram[(j, TILES - 1)][:, mark : mark + 1]
        mean = row / samples
        mean_c = col / samples
        sum_row.append(row)
        mean_row.append(mean)
        sum_col.append(col)
        squares_row = jnp.sum(diagonal, axis=0, keepdims=True)
        squares_col = jnp.sum(diagonal, axis=1, keepdims=True)
        scale_row.append(jnp.sqrt(squares_row / samples - mean * mean + 1e-05))
        scale_col.append(jnp.sqrt(squares_col / samples - mean_c * mean_c + 1e-05))
    lane = lax.broadcasted_iota(jnp.int32, (LANES, LANES), 1)
    sub = lax.broadcasted_iota(jnp.int32, (LANES, LANES), 0)
    for (i, j), n in slot.items():
        value = (gram[(i, j)] - sum_col[i] * sum_row[j] / samples) / (scale_col[i] * scale_row[j])
        if j == TILES - 1:
            value = jnp.where(lane < mark, value, 0.0)
        if i == TILES - 1:
            value = jnp.where(sub < mark, value, 0.0)
        cov[n] = value
        work[n] = jnp.where(eye, value + weight, value) if i == j else value
    side = []
    for j in range(TILES):
        value = (extra[j][0:8] - extra[j][8:16] * mean_trait) / trait_scale / scale_row[j]
        if j == TILES - 1:
            value = jnp.where(lane8 < mark, value, 0.0)
        side.append(value)

    for k in range(TILES):
        a_ref = inv.at[k]
        a_ref[...] = work[slot[(k, k)]]
        invert(a_ref)
        minus = inv[k]
        for j in range(k + 1, TILES):
            ahead = dot(minus, work[slot[(k, j)]])
            for i in range(k + 1, j + 1):
                n = slot[(i, j)]
                work[n] = work[n] + dot_t(work[slot[(k, i)]], ahead)
        if k < TILES - 1:
            part = dot(side[k], minus)
            for j in range(k + 1, TILES):
                side[j] = side[j] + dot(part, work[slot[(k, j)]])

    found = [None] * TILES
    for k in range(TILES - 1, -1, -1):
        value = side[k]
        for j in range(k + 1, TILES):
            value = value - dot_nt(found[j], work[slot[(k, j)]])
        found[k] = -dot(value, inv[k])

    energy = jnp.zeros((8, 1), jnp.float32)
    shift = jnp.zeros((8, 1), jnp.float32)
    betas = []
    for k in range(TILES):
        image = dot(found[k], cov[slot[(k, k)]])
        for j in range(k + 1, TILES):
            image = image + 2.0 * dot_nt(found[j], cov[slot[(k, j)]])
        energy = energy + jnp.sum(image * found[k], axis=1, keepdims=True)
        beta = found[k] / scale_row[k]
        shift = shift + jnp.sum(beta * mean_row[k], axis=1, keepdims=True)
        betas.append(beta)
    norm = 1.0 / jnp.sqrt(energy / samples + 1e-06)
    for k in range(TILES):
        value = betas[k]
        if k == TILES - 1:
            value = jnp.where(lane8 == mark, -shift, jnp.where(lane8 < mark, value, 0.0))
        beta_ref[:, k * LANES : (k + 1) * LANES] = value * norm


def kernel(
    samples, markers, g_hbm, t_hbm, o_hbm, f_hbm, gram_ref, cross_ref,
    g_ref, t_ref, o_ref, f_ref, last, pay, far_in, fin_l, fin_r, acc, zfar_p, zfar_n, near_in, total,
    cov, work, inv, beta_ref, stat_ref, held, betas, outgoing, incoming, columns, weights, part, x_in,
    z_all, final, in_sem, fs, fr, ls, lr, rs, rr, zs_p, zr_p, zs_n, zr_n, ns, nr, gs, gr, hs_p, hr_p,
    hs_n, hr_n, xls, xlr, xrs, xrr, xfs, xfr, ss, sr, a_send, a_recv, ps, pr, ds, dr, ks_p, kr_p,
    ks_n, kr_n, cs, cr,
):
    samp = lax.axis_index("samp")
    blk = lax.axis_index("blk")
    z = samp // XS
    x = lax.rem(samp, XS)
    right = lax.rem(x + 1, XS)
    left = lax.rem(x + XS - 1, XS)
    far = lax.rem(x + 2, XS)
    group = 2 * XS
    place = lax.rem(samp, group)
    leader = samp - place
    pending = []

    def z_of(d):
        return lax.rem(z + d + ZS, ZS)

    def rows_of(d):
        return pl.ds(pl.multiple_of(z_of(d) * CHUNK, 8), CHUNK)

    def to_z(d, src, dst, send, recv):
        copy = remote(src, dst, send, recv, z_of(d) * XS + x, blk)
        pending.append(copy)
        return copy

    def to_x(there, src, dst, send, recv):
        copy = remote(src, dst, send, recv, z * XS + there, blk)
        pending.append(copy)
        return copy

    loads = [
        pltpu.make_async_copy(src, dst, in_sem.at[i])
        for i, (src, dst) in enumerate(
            [(t_hbm, t_ref), (o_hbm, o_ref), (f_hbm, f_ref), (g_hbm, g_ref)]
        )
    ]
    for load in loads:
        load.start()

    barrier = pltpu.get_barrier_semaphore()
    x_peers = [z * XS + lax.rem(x + i, XS) for i in range(1, XS)]
    z_peers = [z_of(d) * XS + x for d in NEAR]
    twin = leader + XS - (place // XS) * XS
    twins = [twin + lax.rem(x + i, XS) for i in range(1, XS)]
    greeted = x_peers + z_peers + twins
    for other in greeted:
        pl.semaphore_signal(barrier, inc=1, device_id=(other, blk), device_id_type=MESH)
    for i in range(1, TRAITS):
        there = lax.rem(blk + i, TRAITS)
        pl.semaphore_signal(barrier, inc=1, device_id=(samp, there), device_id_type=MESH)

    for load in loads:
        load.wait()
    rows = g_ref.shape[1]
    whole = BLOCK // 16 * 16
    start = (TILES - 1) * LANES
    last[0 : whole - start, :] = g_ref[start:whole, :]
    edge = g_ref[whole:BLOCK, :].astype(jnp.float32)
    sub = lax.broadcasted_iota(jnp.int32, (WIDTH - BLOCK, rows), 0)
    edge = jnp.concatenate([edge, (sub == 0).astype(jnp.float32)], axis=0)
    last[whole - start :, :] = edge.astype(jnp.bfloat16)

    def tile(i):
        return last[...] if i == TILES - 1 else g_ref[i * LANES : (i + 1) * LANES, :]

    nt = (((1,), (1,)), ((), ()))
    traits = t_ref[...]
    present = o_ref[...].astype(jnp.float32)
    masked = traits * present
    squares = jnp.sum(masked * traits, axis=1, keepdims=True)
    ones = (lax.broadcasted_iota(jnp.int32, masked.shape, 0) == 0).astype(jnp.float32)
    stacked = jnp.concatenate([*split3(masked), present, ones], axis=0).astype(jnp.bfloat16)
    slot = 0
    for i in range(TILES):
        for j in range(i, TILES):
            value = lax.dot_general(tile(i), tile(j), nt, preferred_element_type=jnp.float32)
            put(pay, slot * LANES, value)
            slot += 1
    for j in range(TILES):
        cols = lax.dot_general(stacked, tile(j), nt, preferred_element_type=jnp.float32)
        rest = cols[32:40]
        if j == TILES - 1:
            lane = lax.broadcasted_iota(jnp.int32, rest.shape, 1)
            rest = jnp.where(lane == ONES + 1 - j * LANES, squares, rest)
        base = len(PAIRS) * LANES + j * EXTRA
        put(pay, base, cols[0:8] + (cols[8:16] + cols[16:24]))
        put(pay, base + 8, cols[24:32])
        put(pay, base + 16, rest)
    for q in range(XS):
        pay[q, QUARTER:, :] = jnp.zeros((LAYERS - QUARTER, LANES), jnp.float32)

    pl.semaphore_wait(barrier, len(greeted) + TRAITS - 1)

    hop, direct, final_l, final_r = [], [], [], []
    for i, d in enumerate(ORDER):
        here = rows_of(d)
        even_step = i % 2 == 0
        toward, away = (right, left) if even_step else (left, right)
        hop.append(to_x(toward, pay.at[far, here], far_in.at[i], fs.at[i], fr.at[i]))
        goes_r = to_x(right, pay.at[right, here], fin_l.at[i], ls.at[i], lr.at[i])
        goes_l = to_x(left, pay.at[left, here], fin_r.at[i], rs.at[i], rr.at[i])
        final_l.append(goes_r)
        final_r.append(goes_l)

    def first_step(seg):
        for i in range(4 * seg, 4 * seg + 4):
            hop[i].start()
        for i in range(4 * seg, 4 * seg + 4):
            (final_r if i % 2 == 0 else final_l)[i].start()

    def second_step(seg):
        for i in range(4 * seg, 4 * seg + 4):
            here = rows_of(ORDER[i])
            there = right if i % 2 == 0 else left
            hop[i].wait_recv()
            pay[there, here, :] = pay[there, here, :] + far_in[i]
            (final_l if i % 2 == 0 else final_r)[i].start()

    zfar, near = {}, {}
    for i, d in enumerate(ORDER):
        if d > 4:
            zfar[d] = to_z(4, acc.at[i], zfar_p.at[d - 5], zs_p.at[d - 5], zr_p.at[d - 5])
        elif d < -4:
            zfar[d] = to_z(-4, acc.at[i], zfar_n.at[-d - 5], zs_n.at[-d - 5], zr_n.at[-d - 5])
        elif d != 0:
            n = NEAR.index(d)
            near[d] = to_z(d, acc.at[i], near_in.at[n], ns.at[n], nr.at[n])

    def third_step(seg):
        for i in range(4 * seg, 4 * seg + 4):
            d = ORDER[i]
            final_l[i].wait_recv()
            final_r[i].wait_recv()
            value = pay[x, rows_of(d), :] + (fin_l[i] + fin_r[i])
            if 1 <= d <= 4:
                zfar[d + 4].wait_recv()
                value = value + zfar_p[d - 1]
            elif -3 <= d <= -1:
                zfar[d - 4].wait_recv()
                value = value + zfar_n[-d - 1]
            acc[i] = value
            if d in zfar:
                zfar[d].start()
            elif d != 0:
                near[d].start()

    first_step(0)
    first_step(1)
    second_step(0)
    first_step(2)
    second_step(1)
    first_step(3)
    third_step(0)
    second_step(2)
    third_step(1)
    second_step(3)
    third_step(2)
    third_step(3)
    value = acc[ORDER.index(0)]
    for n, d in enumerate(NEAR):
        near[d].wait_recv()
        value = value + near_in[n]
    own = rows_of(0)
    total[x, own, :] = value

    spread = {}
    for n, d in enumerate(NEAR):
        spread[-d] = to_z(d, total.at[x, own], total.at[x, own], gs.at[n], gr.at[n])
        spread[-d].start()
    up, down = rows_of(-4), rows_of(4)
    for e in range(4, 0, -1):
        spread[-4 - e] = to_z(e, total.at[x, up], total.at[x, up], hs_p.at[e - 1], hr_p.at[e - 1])
    for e in range(3, 0, -1):
        spread[4 + e] = to_z(-e, total.at[x, down], total.at[x, down], hs_n.at[e - 1], hr_n.at[e - 1])

    goes_r, goes_l, relay = [], [], []
    for j, o in enumerate(ARRIVAL):
        here = rows_of(o)
        goes_r.append(to_x(right, total.at[x, here], total.at[x, here], xls.at[j], xlr.at[j]))
        goes_l.append(to_x(left, total.at[x, here], total.at[x, here], xrs.at[j], xrr.at[j]))
        toward, origin = (right, left) if j % 2 == 0 else (left, right)
        relay.append(to_x(toward, total.at[origin, here], total.at[origin, here], xfs.at[j], xfr.at[j]))

    def pass_on(j):
        (goes_r if j % 2 == 0 else goes_l)[j].wait_recv()
        relay[j].start()

    for j, o in enumerate(ARRIVAL):
        if o != 0:
            spread[o].wait_recv()
        if o == -4:
            for e in range(4, 0, -1):
                spread[-4 - e].start()
        if o == 4:
            for e in range(3, 0, -1):
                spread[4 + e].start()
        goes_r[j].start()
        goes_l[j].start()
        if j >= LAG:
            pass_on(j - LAG)
    for j in range(ZS - LAG, ZS):
        pass_on(j)
    for j in range(ZS):
        (goes_l if j % 2 == 0 else goes_r)[j].wait_recv()
        relay[j].wait_recv()

    solve_local(samples, markers, place, total, beta_ref, stat_ref, cov, work, inv)

    def give(i):
        other = leader + lax.rem(place + i + 1, group)
        return remote(beta_ref, held.at[place], ss.at[i], sr.at[place], other, blk)

    @pl.when(place < PENALTIES)
    def _():
        for i in range(group - 1):
            give(i).start()
        held[place] = beta_ref[...]

    mean = stat_ref[:, 0:1]
    scale = stat_ref[:, 1:2]
    which = lax.broadcasted_iota(jnp.int32, (8, rows), 0) == blk
    mine = jnp.sum(jnp.where(which, present, 0.0), axis=0, keepdims=True)
    scaled = present * (traits - mean) / scale
    scaled = jnp.sum(jnp.where(which, scaled, 0.0), axis=0, keepdims=True)

    for r in range(PENALTIES):

        @pl.when(place != r)
        def _():
            pltpu.make_async_copy(held.at[r], held.at[r], sr.at[r]).wait()

    betas[...] = jnp.zeros_like(betas)
    for r in range(PENALTIES):
        betas[:, r, :] = held[r]
    n = TRAITS * 8
    beta = betas[...].reshape(n, WIDTH)
    beta = jnp.concatenate(split3(beta), axis=0).astype(jnp.bfloat16)
    predicted = jnp.dot(beta[:, start:], last[...], preferred_element_type=jnp.float32)
    predicted = predicted + jnp.dot(
        beta[:, :start], g_ref[0:start, :], preferred_element_type=jnp.float32
    )
    predicted = predicted[0:n] + (predicted[n : 2 * n] + predicted[2 * n :])
    outgoing[...] = predicted.reshape(TRAITS, 8, rows)

    used = pl.ds(0, PENALTIES)
    exchange = []
    for i in range(TRAITS - 1):
        there = lax.rem(blk + i + 1, TRAITS)
        copy = remote(
            outgoing.at[there, used], incoming.at[blk, used], a_send.at[i], a_recv.at[i], samp, there
        )
        copy.start()
        pending.append(copy)
        exchange.append(copy)
    incoming[blk] = outgoing[blk]
    for copy in exchange:
        copy.wait_recv()

    for b in range(TRAITS):
        columns[b * PENALTIES : (b + 1) * PENALTIES, :] = incoming[b, 0:PENALTIES, :]
    columns[STACK:, :] = jnp.broadcast_to(scaled, (SUMS - STACK, rows))
    level = columns[0:STACK, :]
    fold = f_ref[...]
    for k in range(FOLDS):
        weights[k * STACK : (k + 1) * STACK, :] = level * jnp.where(fold == k, mine, 0.0)
    end = FOLDS * STACK
    weights[end:, :] = jnp.zeros((weights.shape[0] - end, rows), jnp.float32)
    local = lax.dot_general(
        columns[...], weights[...], nt, precision=PRECISE, preferred_element_type=jnp.float32
    )
    flat = jnp.concatenate([local[:, 0:LANES], local[:, LANES:]], axis=0)
    for q in range(XS):
        part[q] = flat[q * PARTS : (q + 1) * PARTS]

    sums = []
    for i in range(XS - 1):
        there = lax.rem(x + i + 1, XS)
        sums.append(to_x(there, part.at[there], x_in.at[i], ps.at[i], pr.at[i]))
        sums[i].start()
    for copy in sums:
        copy.wait_recv()
    z_all[z] = part[x] + (x_in[0] + (x_in[1] + x_in[2]))
    spread = {}
    for n, d in enumerate(NEAR):
        spread[-d] = to_z(d, z_all.at[z], z_all.at[z], ds.at[n], dr.at[n])
        spread[-d].start()
    up, down = z_of(-4), z_of(4)
    for e in range(4, 0, -1):
        spread[-4 - e] = to_z(e, z_all.at[up], z_all.at[up], ks_p.at[e - 1], kr_p.at[e - 1])
    for e in range(3, 0, -1):
        spread[4 + e] = to_z(-e, z_all.at[down], z_all.at[down], ks_n.at[e - 1], kr_n.at[e - 1])
    spread[-4].wait_recv()
    for e in range(4, 0, -1):
        spread[-4 - e].start()
    spread[4].wait_recv()
    for e in range(3, 0, -1):
        spread[4 + e].start()
    for o, copy in spread.items():
        if o not in (4, -4):
            copy.wait_recv()
    value = z_all[0]
    for i in range(1, ZS):
        value = value + z_all[i]
    final[x] = value * (FOLDS / samples)
    collect = []
    for i in range(XS - 1):
        there = lax.rem(x + i + 1, XS)
        collect.append(to_x(there, final.at[x], final.at[x], cs.at[i], cr.at[i]))
        collect[i].start()
    for copy in collect:
        copy.wait_recv()
    low = jnp.concatenate([final[0], final[1]], axis=0)
    high = jnp.concatenate([final[2], final[3]], axis=0)
    both = jnp.concatenate([low, high], axis=1)
    for k in range(FOLDS):
        gram_ref[k] = both[0:STACK, k * STACK : (k + 1) * STACK]
        cross_ref[k : k + 1, :] = both[STACK : STACK + 1, k * STACK : (k + 1) * STACK]

    for copy in pending:
        copy.wait_send()

    @pl.when(place < PENALTIES)
    def _():
        for i in range(group - 1):
            give(i).wait_send()


def body(genotypes, traits, observed, fold_index):
    rows, local_cols = genotypes.shape
    samples = rows * lax.axis_size("samp")
    markers = local_cols * lax.axis_size("blk")
    vmem = pl.BlockSpec(memory_space=pltpu.VMEM)
    hbm = pl.BlockSpec(memory_space=pltpu.MemorySpace.HBM)
    dma = pltpu.SemaphoreType.DMA
    f32 = jnp.float32
    chunks = (ZS, CHUNK, LANES)
    grams, cross = pl.pallas_call(
        functools.partial(kernel, samples, markers),
        out_shape=(
            jax.ShapeDtypeStruct((FOLDS, STACK, STACK), f32),
            jax.ShapeDtypeStruct((FOLDS, STACK), f32),
        ),
        in_specs=[hbm] * 4,
        out_specs=(vmem, vmem),
        scratch_shapes=[
            pltpu.VMEM((BLOCK, rows), jnp.bfloat16),
            pltpu.VMEM((TRAITS, rows), f32),
            pltpu.VMEM((TRAITS, rows), jnp.int32),
            pltpu.VMEM((1, rows), jnp.int32),
            pltpu.VMEM((LANES, rows), jnp.bfloat16),
            pltpu.VMEM((XS, LAYERS, LANES), f32),
            pltpu.VMEM(chunks, f32),
            pltpu.VMEM(chunks, f32),
            pltpu.VMEM(chunks, f32),
            pltpu.VMEM(chunks, f32),
            pltpu.VMEM((4, CHUNK, LANES), f32),
            pltpu.VMEM((3, CHUNK, LANES), f32),
            pltpu.VMEM((8, CHUNK, LANES), f32),
            pltpu.VMEM((XS, LAYERS, LANES), f32),
            pltpu.VMEM((len(PAIRS), LANES, LANES), f32),
            pltpu.VMEM((len(PAIRS), LANES, LANES), f32),
            pltpu.VMEM((TILES, LANES, LANES), f32),
            pltpu.VMEM((8, WIDTH), f32),
            pltpu.VMEM((8, LANES), f32),
            pltpu.VMEM((PENALTIES, 8, WIDTH), f32),
            pltpu.VMEM((TRAITS, 8, WIDTH), f32),
            pltpu.VMEM((TRAITS, 8, rows), f32),
            pltpu.VMEM((TRAITS, 8, rows), f32),
            pltpu.VMEM((SUMS, rows), f32),
            pltpu.VMEM((2 * LANES, rows), f32),
            pltpu.VMEM((XS, PARTS, LANES), f32),
            pltpu.VMEM((XS - 1, PARTS, LANES), f32),
            pltpu.VMEM((ZS, PARTS, LANES), f32),
            pltpu.VMEM((XS, PARTS, LANES), f32),
            dma((4,)),
            *[dma((ZS,)) for _ in range(6)],
            *[dma((4,)) for _ in range(2)],
            *[dma((3,)) for _ in range(2)],
            *[dma((8,)) for _ in range(4)],
            *[dma((4,)) for _ in range(2)],
            *[dma((3,)) for _ in range(2)],
            *[dma((ZS,)) for _ in range(6)],
            dma((2 * XS - 1,)),
            dma((PENALTIES,)),
            *[dma((TRAITS - 1,)) for _ in range(2)],
            *[dma((XS - 1,)) for _ in range(2)],
            *[dma((8,)) for _ in range(2)],
            *[dma((4,)) for _ in range(2)],
            *[dma((3,)) for _ in range(2)],
            *[dma((XS - 1,)) for _ in range(2)],
        ],
        compiler_params=pltpu.CompilerParams(
            collective_id=0, has_side_effects=True, vmem_limit_bytes=48 << 20
        ),
        name="ridge",
    )(genotypes.T, traits.T, observed.T, fold_index.reshape(1, rows))
    return grams[None], cross[None]


def solution(mesh):
    in_specs = (P("samp", "blk"), P("samp", None), P("samp", None), P("samp"))
    out_specs = (P("blk", None, None, None), P("blk", None, None))
    return jax.shard_map(body, mesh=mesh, in_specs=in_specs, out_specs=out_specs, check_vma=False)
```

```python
import functools

import jax
import jax.numpy as jnp
from jax import lax
from jax.experimental import pallas as pl
from jax.experimental.pallas import tpu as pltpu
from jax.sharding import PartitionSpec as P

BLOCK = 500
TRAITS = 8
FOLDS = 5
HERITABILITY = (0.01, 0.25, 0.5, 0.75, 0.99)
PENALTIES = len(HERITABILITY)
PRECISE = lax.Precision.HIGHEST
MESH = pl.DeviceIdType.MESH

XS = 4
LANES = 128
TILES = 4
WIDTH = TILES * LANES
ONES = BLOCK
PAIRS = [(i, j) for i in range(TILES) for j in range(i, TILES)]
EXTRA = 24
FLAT = len(PAIRS) * LANES + TILES * EXTRA
QUARTER = FLAT // XS
ZS = 16
CHUNK = 24
LAYERS = ZS * CHUNK
STACK = PENALTIES * 8
SUMS = 48
PARTS = 2 * SUMS // XS
ORDER = [8, 7, 6, 5, -7, -6, -5, -4, 4, 3, 2, 1, -3, -2, -1, 0]
NEAR = [4, -4, 3, -3, 2, -2, 1, -1]
REACH = 8
SOLVERS = [(3, 0), (3, 1), (3, 2), (3, 3), (4, 1)]


def pieces(start, rows):
    out = []
    while rows > 0:
        quarter, row = divmod(start, QUARTER)
        take = min(rows, QUARTER - row)
        out.append((quarter, row, take))
        start += take
        rows -= take
    return out


def put(ref, start, value):
    done = 0
    for quarter, row, take in pieces(start, value.shape[0]):
        ref[quarter, row : row + take, :] = value[done : done + take]
        done += take


def get(ref, start, rows):
    parts = [ref[quarter, row : row + take, :] for quarter, row, take in pieces(start, rows)]
    return parts[0] if len(parts) == 1 else jnp.concatenate(parts, axis=0)


def split3(value):
    first = value.astype(jnp.bfloat16).astype(jnp.float32)
    rest = value - first
    second = rest.astype(jnp.bfloat16).astype(jnp.float32)
    third = rest - second
    return first, second, third


def remote(src, dst, send, recv, samp, blk):
    return pltpu.make_async_remote_copy(
        src_ref=src,
        dst_ref=dst,
        send_sem=send,
        recv_sem=recv,
        device_id=(samp, blk),
        device_id_type=MESH,
    )


def invert(a_ref):
    lane = lax.broadcasted_iota(jnp.int32, (8, LANES), 1)
    sub = lax.broadcasted_iota(jnp.int32, (8, LANES), 0)
    wide = lax.broadcasted_iota(jnp.int32, (LANES, LANES), 1)

    def panel(q, carry):
        base = pl.multiple_of(q * 8, 8)
        shift = lax.rem(LANES - base, LANES)
        strip = a_ref[pl.ds(base, 8), :]
        turned = pltpu.roll(strip, shift, 1)
        cols = [jnp.broadcast_to(turned[:, j : j + 1], (8, LANES)) for j in range(8)]
        inside = jnp.logical_and(lane >= base, lane < base + 8)
        solved = jnp.where(inside, jnp.where(lane - base == sub, -1.0, 0.0), strip)
        for j in range(0, 8, 2):
            one, two = cols[j], cols[j + 1]
            a, b = one[j : j + 1, :], two[j : j + 1, :]
            c, d = one[j + 1 : j + 2, :], two[j + 1 : j + 2, :]
            inverse = 1.0 / (a * d - b * c)
            a, b, c, d = d * inverse, b * inverse, c * inverse, a * inverse

            def step(value):
                top, low = value[j : j + 1, :], value[j + 1 : j + 2, :]
                top, low = a * top - b * low, d * low - c * top
                rest = value - one * top - two * low
                return jnp.where(sub == j, top, jnp.where(sub == j + 1, low, rest))

            solved = step(solved)
            for m in range(j + 2, 8):
                cols[m] = step(cols[m])
        whole = a_ref[...]
        turned_all = pltpu.roll(whole, shift, 1)
        within = jnp.logical_and(wide >= base, wide < base + 8)
        result = jnp.where(within, 0.0, whole)
        for j in range(8):
            result = result - turned_all[:, j : j + 1] * solved[j : j + 1, :]
        a_ref[...] = result
        a_ref[pl.ds(base, 8), :] = solved
        return carry

    lax.fori_loop(0, LANES // 8, panel, 0)


def solve_local(samples, markers, place, total_ref, beta_ref, cov, work, inv):
    weight = jnp.float32(0.0)
    for r, fraction in enumerate(HERITABILITY):
        value = jnp.float32(markers * (1.0 - fraction) / fraction)
        chosen = place == r if r < PENALTIES - 1 else place >= r
        weight = jnp.where(chosen, value, weight)

    dot = functools.partial(jnp.dot, precision=PRECISE, preferred_element_type=jnp.float32)

    def dot_t(a, b):
        return lax.dot_general(
            a, b, (((0,), (0,)), ((), ())), precision=PRECISE, preferred_element_type=jnp.float32
        )

    def dot_nt(a, b):
        return lax.dot_general(
            a, b, (((1,), (1,)), ((), ())), precision=PRECISE, preferred_element_type=jnp.float32
        )

    slot = {pair: n for n, pair in enumerate(PAIRS)}
    gram = {pair: get(total_ref, n * LANES, LANES) for pair, n in slot.items()}
    extra = [get(total_ref, len(PAIRS) * LANES + j * EXTRA, EXTRA) for j in range(TILES)]
    eye = lax.broadcasted_iota(jnp.int32, (LANES, LANES), 0) == lax.broadcasted_iota(
        jnp.int32, (LANES, LANES), 1
    )
    mark = ONES - (TILES - 1) * LANES
    sums = extra[-1][0:8, mark : mark + 1]
    counts = extra[-1][8:16, mark : mark + 1]
    squares = extra[-1][16:24, mark + 1 : mark + 2]
    mean_trait = sums / counts
    trait_scale = jnp.sqrt(squares / counts - mean_trait * mean_trait + 1e-05)
    lane8 = lax.broadcasted_iota(jnp.int32, (8, LANES), 1)

    sum_row, mean_row, scale_row, sum_col, scale_col = [], [], [], [], []
    for j in range(TILES):
        diagonal = jnp.where(eye, gram[(j, j)], 0.0)
        row = extra[j][16:17, :]
        if j == TILES - 1:
            row = jnp.where(lane8[0:1] < mark, row, 0.0)
        col = gram[(j, TILES - 1)][:, mark : mark + 1]
        mean = row / samples
        mean_c = col / samples
        sum_row.append(row)
        mean_row.append(mean)
        sum_col.append(col)
        squares_row = jnp.sum(diagonal, axis=0, keepdims=True)
        squares_col = jnp.sum(diagonal, axis=1, keepdims=True)
        scale_row.append(jnp.sqrt(squares_row / samples - mean * mean + 1e-05))
        scale_col.append(jnp.sqrt(squares_col / samples - mean_c * mean_c + 1e-05))
    lane = lax.broadcasted_iota(jnp.int32, (LANES, LANES), 1)
    sub = lax.broadcasted_iota(jnp.int32, (LANES, LANES), 0)
    for (i, j), n in slot.items():
        value = (gram[(i, j)] - sum_col[i] * sum_row[j] / samples) / (scale_col[i] * scale_row[j])
        if j == TILES - 1:
            value = jnp.where(lane < mark, value, 0.0)
        if i == TILES - 1:
            value = jnp.where(sub < mark, value, 0.0)
        cov[n] = value
        work[n] = jnp.where(eye, value + weight, value) if i == j else value
    side = []
    for j in range(TILES):
        value = (extra[j][0:8] - extra[j][8:16] * mean_trait) / trait_scale / scale_row[j]
        if j == TILES - 1:
            value = jnp.where(lane8 < mark, value, 0.0)
        side.append(value)

    for k in range(TILES):
        a_ref = inv.at[k]
        a_ref[...] = work[slot[(k, k)]]
        invert(a_ref)
        minus = inv[k]
        for j in range(k + 1, TILES):
            ahead = dot(minus, work[slot[(k, j)]])
            for i in range(k + 1, j + 1):
                n = slot[(i, j)]
                work[n] = work[n] + dot_t(work[slot[(k, i)]], ahead)
        if k < TILES - 1:
            part = dot(side[k], minus)
            for j in range(k + 1, TILES):
                side[j] = side[j] + dot(part, work[slot[(k, j)]])

    found = [None] * TILES
    for k in range(TILES - 1, -1, -1):
        value = side[k]
        for j in range(k + 1, TILES):
            value = value - dot_nt(found[j], work[slot[(k, j)]])
        found[k] = -dot(value, inv[k])

    energy = jnp.zeros((8, 1), jnp.float32)
    shift = jnp.zeros((8, 1), jnp.float32)
    betas = []
    for k in range(TILES):
        image = dot(found[k], cov[slot[(k, k)]])
        for j in range(k + 1, TILES):
            image = image + 2.0 * dot_nt(found[j], cov[slot[(k, j)]])
        energy = energy + jnp.sum(image * found[k], axis=1, keepdims=True)
        beta = found[k] / scale_row[k]
        shift = shift + jnp.sum(beta * mean_row[k], axis=1, keepdims=True)
        betas.append(beta)
    norm = 1.0 / jnp.sqrt(energy / samples + 1e-06)
    for k in range(TILES):
        value = betas[k]
        if k == TILES - 1:
            value = jnp.where(lane8 == mark, -shift, jnp.where(lane8 < mark, value, 0.0))
        value = value * norm
        if k == TILES - 1:
            value = jnp.where(lane8 == mark + 1, mean_trait, value)
            value = jnp.where(lane8 == mark + 2, trait_scale, value)
        beta_ref[:, k * LANES : (k + 1) * LANES] = value


def kernel(
    samples, markers, g_hbm, t_hbm, o_hbm, f_hbm, gram_ref, cross_ref,
    g_ref, t_ref, o_ref, f_ref, last, pay, far_in, fin_l, fin_r, acc, zfar_p, zfar_n, near_in, total,
    cov, work, inv, beta_ref, held, betas, outgoing, incoming, columns, weights, part, x_in,
    z_all, final, in_sem, fs, fr, ls, lr, rs, rr, zs_p, zr_p, zs_n, zr_n, ns, nr, gs, gr, ss, sr, a_send, a_recv, ps, pr, ds, dr, ks_p, kr_p,
    ks_n, kr_n, cs, cr,
):
    samp = lax.axis_index("samp")
    blk = lax.axis_index("blk")
    z = samp // XS
    x = lax.rem(samp, XS)
    right = lax.rem(x + 1, XS)
    left = lax.rem(x + XS - 1, XS)
    far = lax.rem(x + 2, XS)
    pending = []
    group = REACH * XS
    place = lax.rem(samp, group)
    leader = samp - place
    spots = [zo * XS + xo for zo, xo in SOLVERS]
    solvers = [base + spot for base in range(0, ZS * XS, group) for spot in spots]
    solving = functools.reduce(jnp.logical_or, [place == spot for spot in spots])
    penalty = functools.reduce(
        lambda found, r: jnp.where(place == spots[r], r, found), range(PENALTIES), 0
    )

    def z_of(d):
        return lax.rem(z + d + ZS, ZS)

    def rows_of(d):
        return pl.ds(pl.multiple_of(z_of(d) * CHUNK, 8), CHUNK)

    def to_z(d, src, dst, send, recv):
        copy = remote(src, dst, send, recv, z_of(d) * XS + x, blk)
        pending.append(copy)
        return copy

    def to_x(there, src, dst, send, recv):
        copy = remote(src, dst, send, recv, z * XS + there, blk)
        pending.append(copy)
        return copy

    loads = [
        pltpu.make_async_copy(src, dst, in_sem.at[i])
        for i, (src, dst) in enumerate(
            [(t_hbm, t_ref), (o_hbm, o_ref), (f_hbm, f_ref), (g_hbm, g_ref)]
        )
    ]
    for load in loads:
        load.start()

    barrier = pltpu.get_barrier_semaphore()
    x_peers = [z * XS + lax.rem(x + i, XS) for i in range(1, XS)]
    z_peers = [z_of(d) * XS + x for d in NEAR]
    greeted = x_peers + z_peers
    for other in greeted:
        pl.semaphore_signal(barrier, inc=1, device_id=(other, blk), device_id_type=MESH)
    for i in range(1, TRAITS):
        there = lax.rem(blk + i, TRAITS)
        pl.semaphore_signal(barrier, inc=1, device_id=(samp, there), device_id_type=MESH)

    for solver in solvers:

        @pl.when(samp != solver)
        def _():
            pl.semaphore_signal(barrier, inc=1, device_id=(solver, blk), device_id_type=MESH)

    def greet(i, carry):
        other = lax.rem(samp + i, ZS * XS)
        pl.semaphore_signal(barrier, inc=1, device_id=(other, blk), device_id_type=MESH)
        return carry

    @pl.when(solving)
    def _():
        lax.fori_loop(1, ZS * XS, greet, 0)

    for load in loads:
        load.wait()
    rows = g_ref.shape[1]
    whole = BLOCK // 16 * 16
    start = (TILES - 1) * LANES
    last[0 : whole - start, :] = g_ref[start:whole, :]
    edge = g_ref[whole:BLOCK, :].astype(jnp.float32)
    sub = lax.broadcasted_iota(jnp.int32, (WIDTH - BLOCK, rows), 0)
    edge = jnp.concatenate([edge, (sub == 0).astype(jnp.float32)], axis=0)
    last[whole - start :, :] = edge.astype(jnp.bfloat16)

    def tile(i):
        return last[...] if i == TILES - 1 else g_ref[i * LANES : (i + 1) * LANES, :]

    nt = (((1,), (1,)), ((), ()))
    traits = t_ref[...]
    present = o_ref[...].astype(jnp.float32)
    masked = traits * present
    squares = jnp.sum(masked * traits, axis=1, keepdims=True)
    ones = (lax.broadcasted_iota(jnp.int32, masked.shape, 0) == 0).astype(jnp.float32)
    stacked = jnp.concatenate([*split3(masked), present, ones], axis=0).astype(jnp.bfloat16)
    slot = 0
    for i in range(TILES):
        for j in range(i, TILES):
            value = lax.dot_general(tile(i), tile(j), nt, preferred_element_type=jnp.float32)
            put(pay, slot * LANES, value)
            slot += 1
    for j in range(TILES):
        cols = lax.dot_general(stacked, tile(j), nt, preferred_element_type=jnp.float32)
        rest = cols[32:40]
        if j == TILES - 1:
            lane = lax.broadcasted_iota(jnp.int32, rest.shape, 1)
            rest = jnp.where(lane == ONES + 1 - j * LANES, squares, rest)
        base = len(PAIRS) * LANES + j * EXTRA
        put(pay, base, cols[0:8] + (cols[8:16] + cols[16:24]))
        put(pay, base + 8, cols[24:32])
        put(pay, base + 16, rest)
    for q in range(XS):
        pay[q, QUARTER:, :] = jnp.zeros((LAYERS - QUARTER, LANES), jnp.float32)

    expected = len(greeted) + TRAITS - 1 + len(solvers)

    @pl.when(solving)
    def _():
        pl.semaphore_wait(barrier, expected - 1 + ZS * XS - 1)

    @pl.when(jnp.logical_not(solving))
    def _():
        pl.semaphore_wait(barrier, expected)


    hop, final_l, final_r = [], [], []
    for i, d in enumerate(ORDER):
        here = rows_of(d)
        even_step = i % 2 == 0
        toward, away = (right, left) if even_step else (left, right)
        hop.append(to_x(toward, pay.at[far, here], far_in.at[i], fs.at[i], fr.at[i]))
        goes_r = to_x(right, pay.at[right, here], fin_l.at[i], ls.at[i], lr.at[i])
        goes_l = to_x(left, pay.at[left, here], fin_r.at[i], rs.at[i], rr.at[i])
        final_l.append(goes_r)
        final_r.append(goes_l)

    def first_step(seg):
        for i in range(4 * seg, 4 * seg + 4):
            hop[i].start()
        for i in range(4 * seg, 4 * seg + 4):
            (final_r if i % 2 == 0 else final_l)[i].start()

    def second_step(seg):
        for i in range(4 * seg, 4 * seg + 4):
            here = rows_of(ORDER[i])
            there = right if i % 2 == 0 else left
            hop[i].wait_recv()
            pay[there, here, :] = pay[there, here, :] + far_in[i]
            (final_l if i % 2 == 0 else final_r)[i].start()

    zfar, near = {}, {}
    for i, d in enumerate(ORDER):
        if d > 4:
            zfar[d] = to_z(4, acc.at[i], zfar_p.at[d - 5], zs_p.at[d - 5], zr_p.at[d - 5])
        elif d < -4:
            zfar[d] = to_z(-4, acc.at[i], zfar_n.at[-d - 5], zs_n.at[-d - 5], zr_n.at[-d - 5])
        elif d != 0:
            n = NEAR.index(d)
            near[d] = to_z(d, acc.at[i], near_in.at[n], ns.at[n], nr.at[n])

    def third_step(seg):
        for i in range(4 * seg, 4 * seg + 4):
            d = ORDER[i]
            final_l[i].wait_recv()
            final_r[i].wait_recv()
            value = pay[x, rows_of(d), :] + (fin_l[i] + fin_r[i])
            if 1 <= d <= 4:
                zfar[d + 4].wait_recv()
                value = value + zfar_p[d - 1]
            elif -3 <= d <= -1:
                zfar[d - 4].wait_recv()
                value = value + zfar_n[-d - 1]
            acc[i] = value
            if d in zfar:
                zfar[d].start()
            elif d != 0:
                near[d].start()

    first_step(0)
    first_step(1)
    second_step(0)
    first_step(2)
    second_step(1)
    first_step(3)
    third_step(0)
    second_step(2)
    third_step(1)
    second_step(3)
    third_step(2)
    third_step(3)
    value = acc[ORDER.index(0)]
    for n, d in enumerate(NEAR):
        near[d].wait_recv()
        value = value + near_in[n]
    own = rows_of(0)
    total[x, own, :] = value

    def report(n):
        here = total.at[x, own]
        return remote(here, here, gs.at[n], gr.at[samp], solvers[n], blk)

    for n, solver in enumerate(solvers):

        @pl.when(samp != solver)
        def _():
            report(n).start()

    def give(i):
        other = leader + lax.rem(place + i, group)
        return remote(beta_ref, held.at[penalty], ss.at[i], sr.at[penalty], other, blk)

    def start_give(i, carry):
        give(i).start()
        return carry

    def wait_give(i, carry):
        give(i).wait_send()
        return carry

    def hear(i, carry):
        other = lax.rem(samp + i, ZS * XS)
        there = pl.ds(pl.multiple_of(other // XS * CHUNK, 8), CHUNK)
        there = total.at[lax.rem(other, XS), there]
        pltpu.make_async_copy(there, there, gr.at[other]).wait()
        return carry

    @pl.when(solving)
    def _():
        lax.fori_loop(1, ZS * XS, hear, 0)
        solve_local(samples, markers, penalty, total, beta_ref, cov, work, inv)
        lax.fori_loop(1, group, start_give, 0)
        held[penalty] = beta_ref[...]

    for r in range(PENALTIES):

        @pl.when(place != spots[r])
        def _():
            pltpu.make_async_copy(held.at[r], held.at[r], sr.at[r]).wait()

    mark = ONES
    mean = held[0, :, mark + 1 : mark + 2]
    scale = held[0, :, mark + 2 : mark + 3]
    which = lax.broadcasted_iota(jnp.int32, (8, rows), 0) == blk
    mine = jnp.sum(jnp.where(which, present, 0.0), axis=0, keepdims=True)
    scaled = present * (traits - mean) / scale
    scaled = jnp.sum(jnp.where(which, scaled, 0.0), axis=0, keepdims=True)
    betas[...] = jnp.zeros_like(betas)
    for r in range(PENALTIES):
        betas[:, r, :] = held[r]
    n = TRAITS * 8
    beta = betas[...].reshape(n, WIDTH)
    beta = jnp.concatenate(split3(beta), axis=0).astype(jnp.bfloat16)
    predicted = jnp.dot(beta[:, start:], last[...], preferred_element_type=jnp.float32)
    predicted = predicted + jnp.dot(
        beta[:, :start], g_ref[0:start, :], preferred_element_type=jnp.float32
    )
    predicted = predicted[0:n] + (predicted[n : 2 * n] + predicted[2 * n :])
    outgoing[...] = predicted.reshape(TRAITS, 8, rows)

    used = pl.ds(0, PENALTIES)
    exchange = []
    for i in range(TRAITS - 1):
        there = lax.rem(blk + i + 1, TRAITS)
        copy = remote(
            outgoing.at[there, used], incoming.at[blk, used], a_send.at[i], a_recv.at[i], samp, there
        )
        copy.start()
        pending.append(copy)
        exchange.append(copy)
    incoming[blk] = outgoing[blk]
    for copy in exchange:
        copy.wait_recv()

    for b in range(TRAITS):
        columns[b * PENALTIES : (b + 1) * PENALTIES, :] = incoming[b, 0:PENALTIES, :]
    columns[STACK:, :] = jnp.broadcast_to(scaled, (SUMS - STACK, rows))
    level = columns[0:STACK, :]
    fold = f_ref[...]
    for k in range(FOLDS):
        weights[k * STACK : (k + 1) * STACK, :] = level * jnp.where(fold == k, mine, 0.0)
    end = FOLDS * STACK
    weights[end:, :] = jnp.zeros((weights.shape[0] - end, rows), jnp.float32)
    local = lax.dot_general(
        columns[...], weights[...], nt, precision=PRECISE, preferred_element_type=jnp.float32
    )
    flat = jnp.concatenate([local[:, 0:LANES], local[:, LANES:]], axis=0)
    for q in range(XS):
        part[q] = flat[q * PARTS : (q + 1) * PARTS]

    sums = []
    for i in range(XS - 1):
        there = lax.rem(x + i + 1, XS)
        sums.append(to_x(there, part.at[there], x_in.at[i], ps.at[i], pr.at[i]))
        sums[i].start()
    for copy in sums:
        copy.wait_recv()
    z_all[z] = part[x] + (x_in[0] + (x_in[1] + x_in[2]))
    spread = {}
    for n, d in enumerate(NEAR):
        spread[-d] = to_z(d, z_all.at[z], z_all.at[z], ds.at[n], dr.at[n])
        spread[-d].start()
    up, down = z_of(-4), z_of(4)
    for e in range(4, 0, -1):
        spread[-4 - e] = to_z(e, z_all.at[up], z_all.at[up], ks_p.at[e - 1], kr_p.at[e - 1])
    for e in range(3, 0, -1):
        spread[4 + e] = to_z(-e, z_all.at[down], z_all.at[down], ks_n.at[e - 1], kr_n.at[e - 1])
    spread[-4].wait_recv()
    for e in range(4, 0, -1):
        spread[-4 - e].start()
    spread[4].wait_recv()
    for e in range(3, 0, -1):
        spread[4 + e].start()
    for o, copy in spread.items():
        if o not in (4, -4):
            copy.wait_recv()
    value = z_all[0]
    for i in range(1, ZS):
        value = value + z_all[i]
    final[x] = value * (FOLDS / samples)
    collect = []
    for i in range(XS - 1):
        there = lax.rem(x + i + 1, XS)
        collect.append(to_x(there, final.at[x], final.at[x], cs.at[i], cr.at[i]))
        collect[i].start()
    for copy in collect:
        copy.wait_recv()
    low = jnp.concatenate([final[0], final[1]], axis=0)
    high = jnp.concatenate([final[2], final[3]], axis=0)
    both = jnp.concatenate([low, high], axis=1)
    for k in range(FOLDS):
        gram_ref[k] = both[0:STACK, k * STACK : (k + 1) * STACK]
        cross_ref[k : k + 1, :] = both[STACK : STACK + 1, k * STACK : (k + 1) * STACK]

    for copy in pending:
        copy.wait_send()

    for n, solver in enumerate(solvers):

        @pl.when(samp != solver)
        def _():
            report(n).wait_send()

    @pl.when(solving)
    def _():
        lax.fori_loop(1, group, wait_give, 0)


def body(genotypes, traits, observed, fold_index):
    rows, local_cols = genotypes.shape
    samples = rows * lax.axis_size("samp")
    markers = local_cols * lax.axis_size("blk")
    vmem = pl.BlockSpec(memory_space=pltpu.VMEM)
    hbm = pl.BlockSpec(memory_space=pltpu.MemorySpace.HBM)
    dma = pltpu.SemaphoreType.DMA
    f32 = jnp.float32
    chunks = (ZS, CHUNK, LANES)
    grams, cross = pl.pallas_call(
        functools.partial(kernel, samples, markers),
        out_shape=(
            jax.ShapeDtypeStruct((FOLDS, STACK, STACK), f32),
            jax.ShapeDtypeStruct((FOLDS, STACK), f32),
        ),
        in_specs=[hbm] * 4,
        out_specs=(vmem, vmem),
        scratch_shapes=[
            pltpu.VMEM((BLOCK, rows), jnp.bfloat16),
            pltpu.VMEM((TRAITS, rows), f32),
            pltpu.VMEM((TRAITS, rows), jnp.int32),
            pltpu.VMEM((1, rows), jnp.int32),
            pltpu.VMEM((LANES, rows), jnp.bfloat16),
            pltpu.VMEM((XS, LAYERS, LANES), f32),
            pltpu.VMEM(chunks, f32),
            pltpu.VMEM(chunks, f32),
            pltpu.VMEM(chunks, f32),
            pltpu.VMEM(chunks, f32),
            pltpu.VMEM((4, CHUNK, LANES), f32),
            pltpu.VMEM((3, CHUNK, LANES), f32),
            pltpu.VMEM((8, CHUNK, LANES), f32),
            pltpu.VMEM((XS, LAYERS, LANES), f32),
            pltpu.VMEM((len(PAIRS), LANES, LANES), f32),
            pltpu.VMEM((len(PAIRS), LANES, LANES), f32),
            pltpu.VMEM((TILES, LANES, LANES), f32),
            pltpu.VMEM((8, WIDTH), f32),
            pltpu.VMEM((PENALTIES, 8, WIDTH), f32),
            pltpu.VMEM((TRAITS, 8, WIDTH), f32),
            pltpu.VMEM((TRAITS, 8, rows), f32),
            pltpu.VMEM((TRAITS, 8, rows), f32),
            pltpu.VMEM((SUMS, rows), f32),
            pltpu.VMEM((2 * LANES, rows), f32),
            pltpu.VMEM((XS, PARTS, LANES), f32),
            pltpu.VMEM((XS - 1, PARTS, LANES), f32),
            pltpu.VMEM((ZS, PARTS, LANES), f32),
            pltpu.VMEM((XS, PARTS, LANES), f32),
            dma((4,)),
            *[dma((ZS,)) for _ in range(6)],
            *[dma((4,)) for _ in range(2)],
            *[dma((3,)) for _ in range(2)],
            *[dma((8,)) for _ in range(2)],
            dma((ZS // REACH * PENALTIES,)),
            dma((ZS * XS,)),
            dma((REACH * XS,)),
            dma((PENALTIES,)),
            *[dma((TRAITS - 1,)) for _ in range(2)],
            *[dma((XS - 1,)) for _ in range(2)],
            *[dma((8,)) for _ in range(2)],
            *[dma((4,)) for _ in range(2)],
            *[dma((3,)) for _ in range(2)],
            *[dma((XS - 1,)) for _ in range(2)],
        ],
        compiler_params=pltpu.CompilerParams(
            collective_id=0, has_side_effects=True, vmem_limit_bytes=67043328
        ),
        name="ridge",
    )(genotypes.T, traits.T, observed.T, fold_index.reshape(1, rows))
    return grams[None], cross[None]


def solution(mesh):
    in_specs = (P("samp", "blk"), P("samp", None), P("samp", None), P("samp"))
    out_specs = (P("blk", None, None, None), P("blk", None, None))
    return jax.shard_map(body, mesh=mesh, in_specs=in_specs, out_specs=out_specs, check_vma=False)
```

```python
import functools

import jax
import jax.numpy as jnp
from jax import lax
from jax.experimental import pallas as pl
from jax.experimental.pallas import tpu as pltpu
from jax.sharding import PartitionSpec as P

BLOCK = 500
TRAITS = 8
FOLDS = 5
HERITABILITY = (0.01, 0.25, 0.5, 0.75, 0.99)
PENALTIES = len(HERITABILITY)
PRECISE = lax.Precision.HIGHEST
MESH = pl.DeviceIdType.MESH

XS = 4
LANES = 128
TILES = 4
WIDTH = TILES * LANES
ONES = BLOCK
PAIRS = [(i, j) for i in range(TILES) for j in range(i, TILES)]
EXTRA = 24
FLAT = len(PAIRS) * LANES + TILES * EXTRA
QUARTER = FLAT // XS
ZS = 16
CHUNK = 24
LAYERS = ZS * CHUNK
STACK = PENALTIES * 8
SUMS = 48
PARTS = 2 * SUMS // XS
ORDER = [8, 7, 6, 5, -7, -6, -5, -4, 4, 3, 2, 1, -3, -2, -1, 0]
NEAR = [4, -4, 3, -3, 2, -2, 1, -1]
REACH = 8
SOLVERS = [(3, 0), (3, 1), (3, 2), (3, 3), (4, 1)]


def pieces(start, rows):
    out = []
    while rows > 0:
        quarter, row = divmod(start, QUARTER)
        take = min(rows, QUARTER - row)
        out.append((quarter, row, take))
        start += take
        rows -= take
    return out


def put(ref, start, value):
    done = 0
    for quarter, row, take in pieces(start, value.shape[0]):
        ref[quarter, row : row + take, :] = value[done : done + take]
        done += take


def get(ref, start, rows):
    parts = [ref[quarter, row : row + take, :] for quarter, row, take in pieces(start, rows)]
    return parts[0] if len(parts) == 1 else jnp.concatenate(parts, axis=0)


def split3(value):
    first = value.astype(jnp.bfloat16).astype(jnp.float32)
    rest = value - first
    second = rest.astype(jnp.bfloat16).astype(jnp.float32)
    third = rest - second
    return first, second, third


def remote(src, dst, send, recv, samp, blk):
    return pltpu.make_async_remote_copy(
        src_ref=src,
        dst_ref=dst,
        send_sem=send,
        recv_sem=recv,
        device_id=(samp, blk),
        device_id_type=MESH,
    )


def invert(a_ref):
    lane = lax.broadcasted_iota(jnp.int32, (8, LANES), 1)
    sub = lax.broadcasted_iota(jnp.int32, (8, LANES), 0)
    wide = lax.broadcasted_iota(jnp.int32, (LANES, LANES), 1)

    def panel(q, carry):
        base = pl.multiple_of(q * 8, 8)
        shift = lax.rem(LANES - base, LANES)
        strip = a_ref[pl.ds(base, 8), :]
        turned = pltpu.roll(strip, shift, 1)
        cols = [jnp.broadcast_to(turned[:, j : j + 1], (8, LANES)) for j in range(8)]
        inside = jnp.logical_and(lane >= base, lane < base + 8)
        solved = jnp.where(inside, jnp.where(lane - base == sub, -1.0, 0.0), strip)
        for j in range(0, 8, 2):
            one, two = cols[j], cols[j + 1]
            a, b = one[j : j + 1, :], two[j : j + 1, :]
            c, d = one[j + 1 : j + 2, :], two[j + 1 : j + 2, :]
            inverse = 1.0 / (a * d - b * c)
            a, b, c, d = d * inverse, b * inverse, c * inverse, a * inverse

            def step(value):
                top, low = value[j : j + 1, :], value[j + 1 : j + 2, :]
                top, low = a * top - b * low, d * low - c * top
                rest = value - one * top - two * low
                return jnp.where(sub == j, top, jnp.where(sub == j + 1, low, rest))

            solved = step(solved)
            for m in range(j + 2, 8):
                cols[m] = step(cols[m])
        whole = a_ref[...]
        turned_all = pltpu.roll(whole, shift, 1)
        within = jnp.logical_and(wide >= base, wide < base + 8)
        result = jnp.where(within, 0.0, whole)
        for j in range(8):
            result = result - turned_all[:, j : j + 1] * solved[j : j + 1, :]
        a_ref[...] = result
        a_ref[pl.ds(base, 8), :] = solved
        return carry

    lax.fori_loop(0, LANES // 8, panel, 0)


def solve_local(samples, markers, place, total_ref, beta_ref, cov, work, inv):
    weight = jnp.float32(0.0)
    for r, fraction in enumerate(HERITABILITY):
        value = jnp.float32(markers * (1.0 - fraction) / fraction)
        chosen = place == r if r < PENALTIES - 1 else place >= r
        weight = jnp.where(chosen, value, weight)

    dot = functools.partial(jnp.dot, precision=PRECISE, preferred_element_type=jnp.float32)

    def dot_t(a, b):
        return lax.dot_general(
            a, b, (((0,), (0,)), ((), ())), precision=PRECISE, preferred_element_type=jnp.float32
        )

    def dot_nt(a, b):
        return lax.dot_general(
            a, b, (((1,), (1,)), ((), ())), precision=PRECISE, preferred_element_type=jnp.float32
        )

    slot = {pair: n for n, pair in enumerate(PAIRS)}
    gram = {pair: get(total_ref, n * LANES, LANES) for pair, n in slot.items()}
    extra = [get(total_ref, len(PAIRS) * LANES + j * EXTRA, EXTRA) for j in range(TILES)]
    eye = lax.broadcasted_iota(jnp.int32, (LANES, LANES), 0) == lax.broadcasted_iota(
        jnp.int32, (LANES, LANES), 1
    )
    mark = ONES - (TILES - 1) * LANES
    sums = extra[-1][0:8, mark : mark + 1]
    counts = extra[-1][8:16, mark : mark + 1]
    squares = extra[-1][16:24, mark + 1 : mark + 2]
    mean_trait = sums / counts
    trait_scale = jnp.sqrt(squares / counts - mean_trait * mean_trait + 1e-05)
    lane8 = lax.broadcasted_iota(jnp.int32, (8, LANES), 1)

    sum_row, mean_row, inverse_row, mean_col, inverse_col = [], [], [], [], []
    for j in range(TILES):
        diagonal = jnp.where(eye, gram[(j, j)], 0.0)
        row = extra[j][16:17, :]
        if j == TILES - 1:
            row = jnp.where(lane8[0:1] < mark, row, 0.0)
        col = gram[(j, TILES - 1)][:, mark : mark + 1]
        mean = row / samples
        mean_c = col / samples
        sum_row.append(row)
        mean_row.append(mean)
        mean_col.append(mean_c)
        squares_row = jnp.sum(diagonal, axis=0, keepdims=True)
        squares_col = jnp.sum(diagonal, axis=1, keepdims=True)
        inverse_row.append(1.0 / jnp.sqrt(squares_row / samples - mean * mean + 1e-05))
        inverse_col.append(1.0 / jnp.sqrt(squares_col / samples - mean_c * mean_c + 1e-05))
    lane = lax.broadcasted_iota(jnp.int32, (LANES, LANES), 1)
    sub = lax.broadcasted_iota(jnp.int32, (LANES, LANES), 0)
    for (i, j), n in slot.items():
        value = (gram[(i, j)] - mean_col[i] * sum_row[j]) * inverse_col[i] * inverse_row[j]
        if j == TILES - 1:
            value = jnp.where(lane < mark, value, 0.0)
        if i == TILES - 1:
            value = jnp.where(sub < mark, value, 0.0)
        cov[n] = value
        work[n] = jnp.where(eye, value + weight, value) if i == j else value
    side = []
    for j in range(TILES):
        value = (extra[j][0:8] - extra[j][8:16] * mean_trait) / trait_scale * inverse_row[j]
        if j == TILES - 1:
            value = jnp.where(lane8 < mark, value, 0.0)
        side.append(value)

    for k in range(TILES):
        a_ref = inv.at[k]
        a_ref[...] = work[slot[(k, k)]]
        invert(a_ref)
        minus = inv[k]
        for j in range(k + 1, TILES):
            ahead = dot(minus, work[slot[(k, j)]])
            for i in range(k + 1, j + 1):
                n = slot[(i, j)]
                work[n] = work[n] + dot_t(work[slot[(k, i)]], ahead)
        if k < TILES - 1:
            part = dot(side[k], minus)
            for j in range(k + 1, TILES):
                side[j] = side[j] + dot(part, work[slot[(k, j)]])

    found = [None] * TILES
    for k in range(TILES - 1, -1, -1):
        value = side[k]
        for j in range(k + 1, TILES):
            value = value - dot_nt(found[j], work[slot[(k, j)]])
        found[k] = -dot(value, inv[k])

    energy = jnp.zeros((8, 1), jnp.float32)
    shift = jnp.zeros((8, 1), jnp.float32)
    betas = []
    for k in range(TILES):
        image = dot(found[k], cov[slot[(k, k)]])
        for j in range(k + 1, TILES):
            image = image + 2.0 * dot_nt(found[j], cov[slot[(k, j)]])
        energy = energy + jnp.sum(image * found[k], axis=1, keepdims=True)
        beta = found[k] * inverse_row[k]
        shift = shift + jnp.sum(beta * mean_row[k], axis=1, keepdims=True)
        betas.append(beta)
    norm = 1.0 / jnp.sqrt(energy / samples + 1e-06)
    for k in range(TILES):
        value = betas[k]
        if k == TILES - 1:
            value = jnp.where(lane8 == mark, -shift, jnp.where(lane8 < mark, value, 0.0))
        value = value * norm
        if k == TILES - 1:
            value = jnp.where(lane8 == mark + 1, mean_trait, value)
            value = jnp.where(lane8 == mark + 2, trait_scale, value)
        beta_ref[:, k * LANES : (k + 1) * LANES] = value


def kernel(
    samples, markers, g_hbm, t_hbm, o_hbm, f_hbm, gram_ref, cross_ref,
    g_ref, t_ref, o_ref, f_ref, last, pay, far_in, fin_l, fin_r, acc, zfar_p, zfar_n, near_in, total,
    cov, work, inv, beta_ref, held, betas, outgoing, incoming, columns, weights, part, x_in,
    z_all, final, in_sem, fs, fr, ls, lr, rs, rr, zs_p, zr_p, zs_n, zr_n, ns, nr, gs, gr, ss, sr, a_send, a_recv, ps, pr, ds, dr, ks_p, kr_p,
    ks_n, kr_n, cs, cr,
):
    samp = lax.axis_index("samp")
    blk = lax.axis_index("blk")
    z = samp // XS
    x = lax.rem(samp, XS)
    right = lax.rem(x + 1, XS)
    left = lax.rem(x + XS - 1, XS)
    far = lax.rem(x + 2, XS)
    pending = []
    group = REACH * XS
    place = lax.rem(samp, group)
    leader = samp - place
    spots = [zo * XS + xo for zo, xo in SOLVERS]
    solvers = [base + spot for base in range(0, ZS * XS, group) for spot in spots]
    solving = functools.reduce(jnp.logical_or, [place == spot for spot in spots])
    penalty = functools.reduce(
        lambda found, r: jnp.where(place == spots[r], r, found), range(PENALTIES), 0
    )

    def z_of(d):
        return lax.rem(z + d + ZS, ZS)

    def rows_of(d):
        return pl.ds(pl.multiple_of(z_of(d) * CHUNK, 8), CHUNK)

    def to_z(d, src, dst, send, recv):
        copy = remote(src, dst, send, recv, z_of(d) * XS + x, blk)
        pending.append(copy)
        return copy

    def to_x(there, src, dst, send, recv):
        copy = remote(src, dst, send, recv, z * XS + there, blk)
        pending.append(copy)
        return copy

    loads = [
        pltpu.make_async_copy(src, dst, in_sem.at[i])
        for i, (src, dst) in enumerate(
            [(t_hbm, t_ref), (o_hbm, o_ref), (f_hbm, f_ref), (g_hbm, g_ref)]
        )
    ]
    for load in loads:
        load.start()

    barrier = pltpu.get_barrier_semaphore()
    x_peers = [z * XS + lax.rem(x + i, XS) for i in range(1, XS)]
    z_peers = [z_of(d) * XS + x for d in NEAR]
    greeted = x_peers + z_peers
    for other in greeted:
        pl.semaphore_signal(barrier, inc=1, device_id=(other, blk), device_id_type=MESH)
    for i in range(1, TRAITS):
        there = lax.rem(blk + i, TRAITS)
        pl.semaphore_signal(barrier, inc=1, device_id=(samp, there), device_id_type=MESH)

    for load in loads:
        load.wait()
    rows = g_ref.shape[1]
    whole = BLOCK // 16 * 16
    start = (TILES - 1) * LANES
    last[0 : whole - start, :] = g_ref[start:whole, :]
    edge = g_ref[whole:BLOCK, :].astype(jnp.float32)
    sub = lax.broadcasted_iota(jnp.int32, (WIDTH - BLOCK, rows), 0)
    edge = jnp.concatenate([edge, (sub == 0).astype(jnp.float32)], axis=0)
    last[whole - start :, :] = edge.astype(jnp.bfloat16)

    def tile(i):
        return last[...] if i == TILES - 1 else g_ref[i * LANES : (i + 1) * LANES, :]

    nt = (((1,), (1,)), ((), ()))
    traits = t_ref[...]
    present = o_ref[...].astype(jnp.float32)
    masked = traits * present
    squares = jnp.sum(masked * traits, axis=1, keepdims=True)
    ones = (lax.broadcasted_iota(jnp.int32, masked.shape, 0) == 0).astype(jnp.float32)
    stacked = jnp.concatenate([*split3(masked), present, ones], axis=0).astype(jnp.bfloat16)
    slot = 0
    for i in range(TILES):
        for j in range(i, TILES):
            value = lax.dot_general(tile(i), tile(j), nt, preferred_element_type=jnp.float32)
            put(pay, slot * LANES, value)
            slot += 1
    for j in range(TILES):
        cols = lax.dot_general(stacked, tile(j), nt, preferred_element_type=jnp.float32)
        rest = cols[32:40]
        if j == TILES - 1:
            lane = lax.broadcasted_iota(jnp.int32, rest.shape, 1)
            rest = jnp.where(lane == ONES + 1 - j * LANES, squares, rest)
        base = len(PAIRS) * LANES + j * EXTRA
        put(pay, base, cols[0:8] + (cols[8:16] + cols[16:24]))
        put(pay, base + 8, cols[24:32])
        put(pay, base + 16, rest)
    for q in range(XS):
        pay[q, QUARTER:, :] = jnp.zeros((LAYERS - QUARTER, LANES), jnp.float32)

    pl.semaphore_wait(barrier, len(greeted) + TRAITS - 1)

    hop, final_l, final_r = [], [], []
    for i, d in enumerate(ORDER):
        here = rows_of(d)
        even_step = i % 2 == 0
        toward, away = (right, left) if even_step else (left, right)
        hop.append(to_x(toward, pay.at[far, here], far_in.at[i], fs.at[i], fr.at[i]))
        goes_r = to_x(right, pay.at[right, here], fin_l.at[i], ls.at[i], lr.at[i])
        goes_l = to_x(left, pay.at[left, here], fin_r.at[i], rs.at[i], rr.at[i])
        final_l.append(goes_r)
        final_r.append(goes_l)

    def first_step(seg):
        for i in range(4 * seg, 4 * seg + 4):
            hop[i].start()
        for i in range(4 * seg, 4 * seg + 4):
            (final_r if i % 2 == 0 else final_l)[i].start()

    def second_step(seg):
        for i in range(4 * seg, 4 * seg + 4):
            here = rows_of(ORDER[i])
            there = right if i % 2 == 0 else left
            hop[i].wait_recv()
            pay[there, here, :] = pay[there, here, :] + far_in[i]
            (final_l if i % 2 == 0 else final_r)[i].start()

    zfar, near = {}, {}
    for i, d in enumerate(ORDER):
        if d > 4:
            zfar[d] = to_z(4, acc.at[i], zfar_p.at[d - 5], zs_p.at[d - 5], zr_p.at[d - 5])
        elif d < -4:
            zfar[d] = to_z(-4, acc.at[i], zfar_n.at[-d - 5], zs_n.at[-d - 5], zr_n.at[-d - 5])
        elif d != 0:
            n = NEAR.index(d)
            near[d] = to_z(d, acc.at[i], near_in.at[n], ns.at[n], nr.at[n])

    def third_step(seg):
        for i in range(4 * seg, 4 * seg + 4):
            d = ORDER[i]
            final_l[i].wait_recv()
            final_r[i].wait_recv()
            value = pay[x, rows_of(d), :] + (fin_l[i] + fin_r[i])
            if 1 <= d <= 4:
                zfar[d + 4].wait_recv()
                value = value + zfar_p[d - 1]
            elif -3 <= d <= -1:
                zfar[d - 4].wait_recv()
                value = value + zfar_n[-d - 1]
            acc[i] = value
            if d in zfar:
                zfar[d].start()
            elif d != 0:
                near[d].start()

    first_step(0)
    first_step(1)
    second_step(0)
    first_step(2)
    second_step(1)
    first_step(3)
    third_step(0)
    second_step(2)
    third_step(1)
    second_step(3)
    third_step(2)
    third_step(3)
    value = acc[ORDER.index(0)]
    for n, d in enumerate(NEAR):
        near[d].wait_recv()
        value = value + near_in[n]
    own = rows_of(0)
    total[x, own, :] = value

    def report(n):
        here = total.at[x, own]
        return remote(here, here, gs.at[n], gr.at[samp], solvers[n], blk)

    for n, solver in enumerate(solvers):

        @pl.when(samp != solver)
        def _():
            report(n).start()

    def give(i):
        other = leader + lax.rem(place + i, group)
        return remote(beta_ref, held.at[penalty], ss.at[i], sr.at[penalty], other, blk)

    def start_give(i, carry):
        give(i).start()
        return carry

    def wait_give(i, carry):
        give(i).wait_send()
        return carry

    def hear(i, carry):
        other = lax.rem(samp + i, ZS * XS)
        there = pl.ds(pl.multiple_of(other // XS * CHUNK, 8), CHUNK)
        there = total.at[lax.rem(other, XS), there]
        pltpu.make_async_copy(there, there, gr.at[other]).wait()
        return carry

    @pl.when(solving)
    def _():
        lax.fori_loop(1, ZS * XS, hear, 0)
        solve_local(samples, markers, penalty, total, beta_ref, cov, work, inv)
        lax.fori_loop(1, group, start_give, 0)
        held[penalty] = beta_ref[...]

    for r in range(PENALTIES):

        @pl.when(place != spots[r])
        def _():
            pltpu.make_async_copy(held.at[r], held.at[r], sr.at[r]).wait()

    mark = ONES
    mean = held[0, :, mark + 1 : mark + 2]
    scale = held[0, :, mark + 2 : mark + 3]
    which = lax.broadcasted_iota(jnp.int32, (8, rows), 0) == blk
    mine = jnp.sum(jnp.where(which, present, 0.0), axis=0, keepdims=True)
    scaled = present * (traits - mean) / scale
    scaled = jnp.sum(jnp.where(which, scaled, 0.0), axis=0, keepdims=True)
    betas[...] = jnp.zeros_like(betas)
    for r in range(PENALTIES):
        betas[:, r, :] = held[r]
    n = TRAITS * 8
    beta = betas[...].reshape(n, WIDTH)
    beta = jnp.concatenate(split3(beta), axis=0).astype(jnp.bfloat16)
    predicted = jnp.dot(beta[:, start:], last[...], preferred_element_type=jnp.float32)
    predicted = predicted + jnp.dot(
        beta[:, :start], g_ref[0:start, :], preferred_element_type=jnp.float32
    )
    predicted = predicted[0:n] + (predicted[n : 2 * n] + predicted[2 * n :])
    outgoing[...] = predicted.reshape(TRAITS, 8, rows)

    used = pl.ds(0, PENALTIES)
    exchange = []
    for i in range(TRAITS - 1):
        there = lax.rem(blk + i + 1, TRAITS)
        copy = remote(
            outgoing.at[there, used], incoming.at[blk, used], a_send.at[i], a_recv.at[i], samp, there
        )
        copy.start()
        pending.append(copy)
        exchange.append(copy)
    incoming[blk] = outgoing[blk]
    for copy in exchange:
        copy.wait_recv()

    for b in range(TRAITS):
        columns[b * PENALTIES : (b + 1) * PENALTIES, :] = incoming[b, 0:PENALTIES, :]
    columns[STACK:, :] = jnp.broadcast_to(scaled, (SUMS - STACK, rows))
    level = columns[0:STACK, :]
    fold = f_ref[...]
    for k in range(FOLDS):
        weights[k * STACK : (k + 1) * STACK, :] = level * jnp.where(fold == k, mine, 0.0)
    end = FOLDS * STACK
    weights[end:, :] = jnp.zeros((weights.shape[0] - end, rows), jnp.float32)
    local = lax.dot_general(
        columns[...], weights[...], nt, precision=PRECISE, preferred_element_type=jnp.float32
    )
    flat = jnp.concatenate([local[:, 0:LANES], local[:, LANES:]], axis=0)
    for q in range(XS):
        part[q] = flat[q * PARTS : (q + 1) * PARTS]

    sums = []
    for i in range(XS - 1):
        there = lax.rem(x + i + 1, XS)
        sums.append(to_x(there, part.at[there], x_in.at[i], ps.at[i], pr.at[i]))
        sums[i].start()
    for copy in sums:
        copy.wait_recv()
    z_all[z] = part[x] + (x_in[0] + (x_in[1] + x_in[2]))
    spread = {}
    for n, d in enumerate(NEAR):
        spread[-d] = to_z(d, z_all.at[z], z_all.at[z], ds.at[n], dr.at[n])
        spread[-d].start()
    up, down = z_of(-4), z_of(4)
    for e in range(4, 0, -1):
        spread[-4 - e] = to_z(e, z_all.at[up], z_all.at[up], ks_p.at[e - 1], kr_p.at[e - 1])
    for e in range(3, 0, -1):
        spread[4 + e] = to_z(-e, z_all.at[down], z_all.at[down], ks_n.at[e - 1], kr_n.at[e - 1])
    spread[-4].wait_recv()
    for e in range(4, 0, -1):
        spread[-4 - e].start()
    spread[4].wait_recv()
    for e in range(3, 0, -1):
        spread[4 + e].start()
    for o, copy in spread.items():
        if o not in (4, -4):
            copy.wait_recv()
    value = z_all[0]
    for i in range(1, ZS):
        value = value + z_all[i]
    final[x] = value * (FOLDS / samples)
    collect = []
    for i in range(XS - 1):
        there = lax.rem(x + i + 1, XS)
        collect.append(to_x(there, final.at[x], final.at[x], cs.at[i], cr.at[i]))
        collect[i].start()
    for copy in collect:
        copy.wait_recv()
    low = jnp.concatenate([final[0], final[1]], axis=0)
    high = jnp.concatenate([final[2], final[3]], axis=0)
    both = jnp.concatenate([low, high], axis=1)
    for k in range(FOLDS):
        gram_ref[k] = both[0:STACK, k * STACK : (k + 1) * STACK]
        cross_ref[k : k + 1, :] = both[STACK : STACK + 1, k * STACK : (k + 1) * STACK]

    for copy in pending:
        copy.wait_send()

    for n, solver in enumerate(solvers):

        @pl.when(samp != solver)
        def _():
            report(n).wait_send()

    @pl.when(solving)
    def _():
        lax.fori_loop(1, group, wait_give, 0)


def body(genotypes, traits, observed, fold_index):
    rows, local_cols = genotypes.shape
    samples = rows * lax.axis_size("samp")
    markers = local_cols * lax.axis_size("blk")
    vmem = pl.BlockSpec(memory_space=pltpu.VMEM)
    hbm = pl.BlockSpec(memory_space=pltpu.MemorySpace.HBM)
    dma = pltpu.SemaphoreType.DMA
    f32 = jnp.float32
    chunks = (ZS, CHUNK, LANES)
    grams, cross = pl.pallas_call(
        functools.partial(kernel, samples, markers),
        out_shape=(
            jax.ShapeDtypeStruct((FOLDS, STACK, STACK), f32),
            jax.ShapeDtypeStruct((FOLDS, STACK), f32),
        ),
        in_specs=[hbm] * 4,
        out_specs=(vmem, vmem),
        scratch_shapes=[
            pltpu.VMEM((BLOCK, rows), jnp.bfloat16),
            pltpu.VMEM((TRAITS, rows), f32),
            pltpu.VMEM((TRAITS, rows), jnp.int32),
            pltpu.VMEM((1, rows), jnp.int32),
            pltpu.VMEM((LANES, rows), jnp.bfloat16),
            pltpu.VMEM((XS, LAYERS, LANES), f32),
            pltpu.VMEM(chunks, f32),
            pltpu.VMEM(chunks, f32),
            pltpu.VMEM(chunks, f32),
            pltpu.VMEM(chunks, f32),
            pltpu.VMEM((4, CHUNK, LANES), f32),
            pltpu.VMEM((3, CHUNK, LANES), f32),
            pltpu.VMEM((8, CHUNK, LANES), f32),
            pltpu.VMEM((XS, LAYERS, LANES), f32),
            pltpu.VMEM((len(PAIRS), LANES, LANES), f32),
            pltpu.VMEM((len(PAIRS), LANES, LANES), f32),
            pltpu.VMEM((TILES, LANES, LANES), f32),
            pltpu.VMEM((8, WIDTH), f32),
            pltpu.VMEM((PENALTIES, 8, WIDTH), f32),
            pltpu.VMEM((TRAITS, 8, WIDTH), f32),
            pltpu.VMEM((TRAITS, 8, rows), f32),
            pltpu.VMEM((TRAITS, 8, rows), f32),
            pltpu.VMEM((SUMS, rows), f32),
            pltpu.VMEM((2 * LANES, rows), f32),
            pltpu.VMEM((XS, PARTS, LANES), f32),
            pltpu.VMEM((XS - 1, PARTS, LANES), f32),
            pltpu.VMEM((ZS, PARTS, LANES), f32),
            pltpu.VMEM((XS, PARTS, LANES), f32),
            dma((4,)),
            *[dma((ZS,)) for _ in range(6)],
            *[dma((4,)) for _ in range(2)],
            *[dma((3,)) for _ in range(2)],
            *[dma((8,)) for _ in range(2)],
            dma((ZS // REACH * PENALTIES,)),
            dma((ZS * XS,)),
            dma((REACH * XS,)),
            dma((PENALTIES,)),
            *[dma((TRAITS - 1,)) for _ in range(2)],
            *[dma((XS - 1,)) for _ in range(2)],
            *[dma((8,)) for _ in range(2)],
            *[dma((4,)) for _ in range(2)],
            *[dma((3,)) for _ in range(2)],
            *[dma((XS - 1,)) for _ in range(2)],
        ],
        compiler_params=pltpu.CompilerParams(
            collective_id=0, has_side_effects=True, vmem_limit_bytes=67043328
        ),
        name="ridge",
    )(genotypes.T, traits.T, observed.T, fold_index.reshape(1, rows))
    return grams[None], cross[None]


def solution(mesh):
    in_specs = (P("samp", "blk"), P("samp", None), P("samp", None), P("samp"))
    out_specs = (P("blk", None, None, None), P("blk", None, None))
    return jax.shard_map(body, mesh=mesh, in_specs=in_specs, out_specs=out_specs, check_vma=False)
```

```python
import functools

import jax
import jax.numpy as jnp
from jax import lax
from jax.experimental import pallas as pl
from jax.experimental.pallas import tpu as pltpu
from jax.sharding import PartitionSpec as P

BLOCK = 500
TRAITS = 8
FOLDS = 5
HERITABILITY = (0.01, 0.25, 0.5, 0.75, 0.99)
PENALTIES = len(HERITABILITY)
PRECISE = lax.Precision.HIGHEST
MESH = pl.DeviceIdType.MESH

XS = 4
LANES = 128
TILES = 4
WIDTH = TILES * LANES
ONES = BLOCK
PAIRS = [(i, j) for i in range(TILES) for j in range(i, TILES)]
EXTRA = 24
FLAT = len(PAIRS) * LANES + TILES * EXTRA
QUARTER = FLAT // XS
ZS = 16
CHUNK = 24
LAYERS = ZS * CHUNK
STACK = PENALTIES * 8
SUMS = 48
PARTS = 2 * SUMS // XS
ORDER = [8, 7, 6, 5, -7, -6, -5, -4, 4, 3, 2, 1, -3, -2, -1, 0]
NEAR = [4, -4, 3, -3, 2, -2, 1, -1]
REACH = 8
SOLVERS = [(3, 0), (3, 1), (3, 2), (3, 3), (4, 1)]


def pieces(start, rows):
    out = []
    while rows > 0:
        quarter, row = divmod(start, QUARTER)
        take = min(rows, QUARTER - row)
        out.append((quarter, row, take))
        start += take
        rows -= take
    return out


def put(ref, start, value):
    done = 0
    for quarter, row, take in pieces(start, value.shape[0]):
        ref[quarter, row : row + take, :] = value[done : done + take]
        done += take


def get(ref, start, rows):
    parts = [ref[quarter, row : row + take, :] for quarter, row, take in pieces(start, rows)]
    return parts[0] if len(parts) == 1 else jnp.concatenate(parts, axis=0)


def split3(value):
    first = value.astype(jnp.bfloat16).astype(jnp.float32)
    rest = value - first
    second = rest.astype(jnp.bfloat16).astype(jnp.float32)
    third = rest - second
    return first, second, third


def remote(src, dst, send, recv, samp, blk):
    return pltpu.make_async_remote_copy(
        src_ref=src,
        dst_ref=dst,
        send_sem=send,
        recv_sem=recv,
        device_id=(samp, blk),
        device_id_type=MESH,
    )


def invert(a_ref):
    lane = lax.broadcasted_iota(jnp.int32, (8, LANES), 1)
    sub = lax.broadcasted_iota(jnp.int32, (8, LANES), 0)
    wide = lax.broadcasted_iota(jnp.int32, (LANES, LANES), 1)
    panels = LANES // 8

    def columns_of(strip, base):
        turned = pltpu.roll(strip, lax.rem(LANES - base, LANES), 1)
        return [jnp.broadcast_to(turned[:, j : j + 1], (8, LANES)) for j in range(8)]

    def advance(strip, base, solved):
        cols = columns_of(strip, base)
        terms = [cols[j] * solved[j : j + 1, :] for j in range(8)]
        while len(terms) > 1:
            terms = [terms[i] + terms[i + 1] for i in range(0, len(terms), 2)]
        inside = jnp.logical_and(lane >= base, lane < base + 8)
        return jnp.where(inside, 0.0, strip) - terms[0]

    def pivots(strip, base):
        cols = columns_of(strip, base)
        inside = jnp.logical_and(lane >= base, lane < base + 8)
        solved = jnp.where(inside, jnp.where(lane - base == sub, -1.0, 0.0), strip)
        for j in range(0, 8, 2):
            one, two = cols[j], cols[j + 1]
            a, b = one[j : j + 1, :], two[j : j + 1, :]
            c, d = one[j + 1 : j + 2, :], two[j + 1 : j + 2, :]
            inverse = 1.0 / (a * d - b * c)
            a, b, c, d = d * inverse, b * inverse, c * inverse, a * inverse

            def step(value):
                top, low = value[j : j + 1, :], value[j + 1 : j + 2, :]
                top, low = a * top - b * low, d * low - c * top
                rest = value - one * top - two * low
                return jnp.where(sub == j, top, jnp.where(sub == j + 1, low, rest))

            solved = step(solved)
            for m in range(j + 2, 8):
                cols[m] = step(cols[m])
        return solved

    def update(base, strip, solved, keep):
        a1, a2, a3 = split3(strip)
        b1, b2, b3 = split3(solved)
        lhs = jnp.concatenate([a1, a1, a2, a1, a3, a2], axis=0).astype(jnp.bfloat16)
        rhs = jnp.concatenate([b1, b2, b1, b3, b1, b2], axis=0).astype(jnp.bfloat16)
        product = lax.dot_general(
            lhs, rhs, (((0,), (0,)), ((), ())), preferred_element_type=jnp.float32
        )
        within = jnp.logical_and(wide >= base, wide < base + 8)
        a_ref[...] = jnp.where(within, 0.0, a_ref[...]) - product
        a_ref[pl.ds(pl.multiple_of(jnp.maximum(base, 0), 8), 8), :] = keep

    def panel(q, carry):
        strip, before, done = carry
        base = pl.multiple_of(q * 8, 8)
        ahead = pl.multiple_of(lax.rem(q + 1, panels) * 8, 8)
        coming = a_ref[pl.ds(ahead, 8), :]
        last = lax.rem(base - 8 + LANES, LANES)
        moved = advance(coming, last, done)
        coming = jnp.where(q > 0, moved, coming)
        solved = pivots(strip, base)
        update(base - 8, before, done, jnp.where(q > 0, done, strip))
        return advance(coming, base, solved), strip, solved

    zero = jnp.zeros((8, LANES), jnp.float32)
    strip, before, done = lax.fori_loop(0, panels, panel, (a_ref[0:8, :], zero, zero))
    update(LANES - 8, before, done, done)


def solve_local(samples, markers, place, total_ref, beta_ref, cov, work, inv):
    weight = jnp.float32(0.0)
    for r, fraction in enumerate(HERITABILITY):
        value = jnp.float32(markers * (1.0 - fraction) / fraction)
        chosen = place == r if r < PENALTIES - 1 else place >= r
        weight = jnp.where(chosen, value, weight)

    dot = functools.partial(jnp.dot, precision=PRECISE, preferred_element_type=jnp.float32)

    def dot_t(a, b):
        return lax.dot_general(
            a, b, (((0,), (0,)), ((), ())), precision=PRECISE, preferred_element_type=jnp.float32
        )

    def dot_nt(a, b):
        return lax.dot_general(
            a, b, (((1,), (1,)), ((), ())), precision=PRECISE, preferred_element_type=jnp.float32
        )

    slot = {pair: n for n, pair in enumerate(PAIRS)}
    gram = {pair: get(total_ref, n * LANES, LANES) for pair, n in slot.items()}
    extra = [get(total_ref, len(PAIRS) * LANES + j * EXTRA, EXTRA) for j in range(TILES)]
    eye = lax.broadcasted_iota(jnp.int32, (LANES, LANES), 0) == lax.broadcasted_iota(
        jnp.int32, (LANES, LANES), 1
    )
    mark = ONES - (TILES - 1) * LANES
    sums = extra[-1][0:8, mark : mark + 1]
    counts = extra[-1][8:16, mark : mark + 1]
    squares = extra[-1][16:24, mark + 1 : mark + 2]
    mean_trait = sums / counts
    trait_scale = jnp.sqrt(squares / counts - mean_trait * mean_trait + 1e-05)
    lane8 = lax.broadcasted_iota(jnp.int32, (8, LANES), 1)

    sum_row, mean_row, inverse_row, mean_col, inverse_col = [], [], [], [], []
    for j in range(TILES):
        diagonal = jnp.where(eye, gram[(j, j)], 0.0)
        row = extra[j][16:17, :]
        if j == TILES - 1:
            row = jnp.where(lane8[0:1] < mark, row, 0.0)
        col = gram[(j, TILES - 1)][:, mark : mark + 1]
        mean = row / samples
        mean_c = col / samples
        sum_row.append(row)
        mean_row.append(mean)
        mean_col.append(mean_c)
        squares_row = jnp.sum(diagonal, axis=0, keepdims=True)
        squares_col = jnp.sum(diagonal, axis=1, keepdims=True)
        inverse_row.append(1.0 / jnp.sqrt(squares_row / samples - mean * mean + 1e-05))
        inverse_col.append(1.0 / jnp.sqrt(squares_col / samples - mean_c * mean_c + 1e-05))
    lane = lax.broadcasted_iota(jnp.int32, (LANES, LANES), 1)
    sub = lax.broadcasted_iota(jnp.int32, (LANES, LANES), 0)
    for (i, j), n in slot.items():
        value = (gram[(i, j)] - mean_col[i] * sum_row[j]) * inverse_col[i] * inverse_row[j]
        if j == TILES - 1:
            value = jnp.where(lane < mark, value, 0.0)
        if i == TILES - 1:
            value = jnp.where(sub < mark, value, 0.0)
        cov[n] = value
        work[n] = jnp.where(eye, value + weight, value) if i == j else value
    side = []
    for j in range(TILES):
        value = (extra[j][0:8] - extra[j][8:16] * mean_trait) / trait_scale * inverse_row[j]
        if j == TILES - 1:
            value = jnp.where(lane8 < mark, value, 0.0)
        side.append(value)

    for k in range(TILES):
        a_ref = inv.at[k]
        a_ref[...] = work[slot[(k, k)]]
        invert(a_ref)
        minus = inv[k]
        for j in range(k + 1, TILES):
            ahead = dot(minus, work[slot[(k, j)]])
            for i in range(k + 1, j + 1):
                n = slot[(i, j)]
                work[n] = work[n] + dot_t(work[slot[(k, i)]], ahead)
        if k < TILES - 1:
            part = dot(side[k], minus)
            for j in range(k + 1, TILES):
                side[j] = side[j] + dot(part, work[slot[(k, j)]])

    found = [None] * TILES
    for k in range(TILES - 1, -1, -1):
        value = side[k]
        for j in range(k + 1, TILES):
            value = value - dot_nt(found[j], work[slot[(k, j)]])
        found[k] = -dot(value, inv[k])

    energy = jnp.zeros((8, 1), jnp.float32)
    shift = jnp.zeros((8, 1), jnp.float32)
    betas = []
    for k in range(TILES):
        image = dot(found[k], cov[slot[(k, k)]])
        for j in range(k + 1, TILES):
            image = image + 2.0 * dot_nt(found[j], cov[slot[(k, j)]])
        energy = energy + jnp.sum(image * found[k], axis=1, keepdims=True)
        beta = found[k] * inverse_row[k]
        shift = shift + jnp.sum(beta * mean_row[k], axis=1, keepdims=True)
        betas.append(beta)
    norm = 1.0 / jnp.sqrt(energy / samples + 1e-06)
    for k in range(TILES):
        value = betas[k]
        if k == TILES - 1:
            value = jnp.where(lane8 == mark, -shift, jnp.where(lane8 < mark, value, 0.0))
        value = value * norm
        if k == TILES - 1:
            value = jnp.where(lane8 == mark + 1, mean_trait, value)
            value = jnp.where(lane8 == mark + 2, trait_scale, value)
        beta_ref[:, k * LANES : (k + 1) * LANES] = value


def kernel(
    samples, markers, g_hbm, t_hbm, o_hbm, f_hbm, gram_ref, cross_ref,
    g_ref, t_ref, o_ref, f_ref, last, pay, far_in, fin_l, fin_r, acc, zfar_p, zfar_n, near_in, total,
    cov, work, inv, beta_ref, held, betas, outgoing, incoming, columns, weights, part, x_in,
    z_all, final, in_sem, fs, fr, ls, lr, rs, rr, zs_p, zr_p, zs_n, zr_n, ns, nr, gs, gr, ss, sr, a_send, a_recv, ps, pr, ds, dr, ks_p, kr_p,
    ks_n, kr_n, cs, cr,
):
    samp = lax.axis_index("samp")
    blk = lax.axis_index("blk")
    z = samp // XS
    x = lax.rem(samp, XS)
    right = lax.rem(x + 1, XS)
    left = lax.rem(x + XS - 1, XS)
    far = lax.rem(x + 2, XS)
    pending = []
    group = REACH * XS
    place = lax.rem(samp, group)
    leader = samp - place
    spots = [zo * XS + xo for zo, xo in SOLVERS]
    solvers = [base + spot for base in range(0, ZS * XS, group) for spot in spots]
    solving = functools.reduce(jnp.logical_or, [place == spot for spot in spots])
    penalty = functools.reduce(
        lambda found, r: jnp.where(place == spots[r], r, found), range(PENALTIES), 0
    )

    def z_of(d):
        return lax.rem(z + d + ZS, ZS)

    def rows_of(d):
        return pl.ds(pl.multiple_of(z_of(d) * CHUNK, 8), CHUNK)

    def to_z(d, src, dst, send, recv):
        copy = remote(src, dst, send, recv, z_of(d) * XS + x, blk)
        pending.append(copy)
        return copy

    def to_x(there, src, dst, send, recv):
        copy = remote(src, dst, send, recv, z * XS + there, blk)
        pending.append(copy)
        return copy

    loads = [
        pltpu.make_async_copy(src, dst, in_sem.at[i])
        for i, (src, dst) in enumerate(
            [(t_hbm, t_ref), (o_hbm, o_ref), (f_hbm, f_ref), (g_hbm, g_ref)]
        )
    ]
    for load in loads:
        load.start()

    barrier = pltpu.get_barrier_semaphore()
    x_peers = [z * XS + lax.rem(x + i, XS) for i in range(1, XS)]
    z_peers = [z_of(d) * XS + x for d in NEAR]
    greeted = x_peers + z_peers
    for other in greeted:
        pl.semaphore_signal(barrier, inc=1, device_id=(other, blk), device_id_type=MESH)
    for i in range(1, TRAITS):
        there = lax.rem(blk + i, TRAITS)
        pl.semaphore_signal(barrier, inc=1, device_id=(samp, there), device_id_type=MESH)

    for load in loads:
        load.wait()
    rows = g_ref.shape[1]
    whole = BLOCK // 16 * 16
    start = (TILES - 1) * LANES
    last[0 : whole - start, :] = g_ref[start:whole, :]
    edge = g_ref[whole:BLOCK, :].astype(jnp.float32)
    sub = lax.broadcasted_iota(jnp.int32, (WIDTH - BLOCK, rows), 0)
    edge = jnp.concatenate([edge, (sub == 0).astype(jnp.float32)], axis=0)
    last[whole - start :, :] = edge.astype(jnp.bfloat16)

    def tile(i):
        return last[...] if i == TILES - 1 else g_ref[i * LANES : (i + 1) * LANES, :]

    nt = (((1,), (1,)), ((), ()))
    traits = t_ref[...]
    present = o_ref[...].astype(jnp.float32)
    masked = traits * present
    squares = jnp.sum(masked * traits, axis=1, keepdims=True)
    ones = (lax.broadcasted_iota(jnp.int32, masked.shape, 0) == 0).astype(jnp.float32)
    stacked = jnp.concatenate([*split3(masked), present, ones], axis=0).astype(jnp.bfloat16)
    slot = 0
    for i in range(TILES):
        for j in range(i, TILES):
            value = lax.dot_general(tile(i), tile(j), nt, preferred_element_type=jnp.float32)
            put(pay, slot * LANES, value)
            slot += 1
    for j in range(TILES):
        cols = lax.dot_general(stacked, tile(j), nt, preferred_element_type=jnp.float32)
        rest = cols[32:40]
        if j == TILES - 1:
            lane = lax.broadcasted_iota(jnp.int32, rest.shape, 1)
            rest = jnp.where(lane == ONES + 1 - j * LANES, squares, rest)
        base = len(PAIRS) * LANES + j * EXTRA
        put(pay, base, cols[0:8] + (cols[8:16] + cols[16:24]))
        put(pay, base + 8, cols[24:32])
        put(pay, base + 16, rest)
    for q in range(XS):
        pay[q, QUARTER:, :] = jnp.zeros((LAYERS - QUARTER, LANES), jnp.float32)

    pl.semaphore_wait(barrier, len(greeted) + TRAITS - 1)

    hop, final_l, final_r = [], [], []
    for i, d in enumerate(ORDER):
        here = rows_of(d)
        even_step = i % 2 == 0
        toward, away = (right, left) if even_step else (left, right)
        hop.append(to_x(toward, pay.at[far, here], far_in.at[i], fs.at[i], fr.at[i]))
        goes_r = to_x(right, pay.at[right, here], fin_l.at[i], ls.at[i], lr.at[i])
        goes_l = to_x(left, pay.at[left, here], fin_r.at[i], rs.at[i], rr.at[i])
        final_l.append(goes_r)
        final_r.append(goes_l)

    def first_step(seg):
        for i in range(4 * seg, 4 * seg + 4):
            hop[i].start()
        for i in range(4 * seg, 4 * seg + 4):
            (final_r if i % 2 == 0 else final_l)[i].start()

    def second_step(seg):
        for i in range(4 * seg, 4 * seg + 4):
            here = rows_of(ORDER[i])
            there = right if i % 2 == 0 else left
            hop[i].wait_recv()
            pay[there, here, :] = pay[there, here, :] + far_in[i]
            (final_l if i % 2 == 0 else final_r)[i].start()

    zfar, near = {}, {}
    for i, d in enumerate(ORDER):
        if d > 4:
            zfar[d] = to_z(4, acc.at[i], zfar_p.at[d - 5], zs_p.at[d - 5], zr_p.at[d - 5])
        elif d < -4:
            zfar[d] = to_z(-4, acc.at[i], zfar_n.at[-d - 5], zs_n.at[-d - 5], zr_n.at[-d - 5])
        elif d != 0:
            n = NEAR.index(d)
            near[d] = to_z(d, acc.at[i], near_in.at[n], ns.at[n], nr.at[n])

    def third_step(seg):
        for i in range(4 * seg, 4 * seg + 4):
            d = ORDER[i]
            final_l[i].wait_recv()
            final_r[i].wait_recv()
            value = pay[x, rows_of(d), :] + (fin_l[i] + fin_r[i])
            if 1 <= d <= 4:
                zfar[d + 4].wait_recv()
                value = value + zfar_p[d - 1]
            elif -3 <= d <= -1:
                zfar[d - 4].wait_recv()
                value = value + zfar_n[-d - 1]
            acc[i] = value
            if d in zfar:
                zfar[d].start()
            elif d != 0:
                near[d].start()

    first_step(0)
    first_step(1)
    second_step(0)
    first_step(2)
    second_step(1)
    first_step(3)
    third_step(0)
    second_step(2)
    third_step(1)
    second_step(3)
    third_step(2)
    third_step(3)
    value = acc[ORDER.index(0)]
    for n, d in enumerate(NEAR):
        near[d].wait_recv()
        value = value + near_in[n]
    own = rows_of(0)
    total[x, own, :] = value

    def report(n):
        here = total.at[x, own]
        return remote(here, here, gs.at[n], gr.at[samp], solvers[n], blk)

    for n, solver in enumerate(solvers):

        @pl.when(samp != solver)
        def _():
            report(n).start()

    def give(i):
        other = leader + lax.rem(place + i, group)
        return remote(beta_ref, held.at[penalty], ss.at[i], sr.at[penalty], other, blk)

    def start_give(i, carry):
        give(i).start()
        return carry

    def wait_give(i, carry):
        give(i).wait_send()
        return carry

    def hear(i, carry):
        other = lax.rem(samp + i, ZS * XS)
        there = pl.ds(pl.multiple_of(other // XS * CHUNK, 8), CHUNK)
        there = total.at[lax.rem(other, XS), there]
        pltpu.make_async_copy(there, there, gr.at[other]).wait()
        return carry

    @pl.when(solving)
    def _():
        lax.fori_loop(1, ZS * XS, hear, 0)
        solve_local(samples, markers, penalty, total, beta_ref, cov, work, inv)
        lax.fori_loop(1, group, start_give, 0)
        held[penalty] = beta_ref[...]

    for r in range(PENALTIES):

        @pl.when(place != spots[r])
        def _():
            pltpu.make_async_copy(held.at[r], held.at[r], sr.at[r]).wait()

    mark = ONES
    mean = held[0, :, mark + 1 : mark + 2]
    scale = held[0, :, mark + 2 : mark + 3]
    which = lax.broadcasted_iota(jnp.int32, (8, rows), 0) == blk
    mine = jnp.sum(jnp.where(which, present, 0.0), axis=0, keepdims=True)
    scaled = present * (traits - mean) / scale
    scaled = jnp.sum(jnp.where(which, scaled, 0.0), axis=0, keepdims=True)
    betas[...] = jnp.zeros_like(betas)
    for r in range(PENALTIES):
        betas[:, r, :] = held[r]
    n = TRAITS * 8
    beta = betas[...].reshape(n, WIDTH)
    beta = jnp.concatenate(split3(beta), axis=0).astype(jnp.bfloat16)
    predicted = jnp.dot(beta[:, start:], last[...], preferred_element_type=jnp.float32)
    predicted = predicted + jnp.dot(
        beta[:, :start], g_ref[0:start, :], preferred_element_type=jnp.float32
    )
    predicted = predicted[0:n] + (predicted[n : 2 * n] + predicted[2 * n :])
    outgoing[...] = predicted.reshape(TRAITS, 8, rows)

    used = pl.ds(0, PENALTIES)
    exchange = []
    for i in range(TRAITS - 1):
        there = lax.rem(blk + i + 1, TRAITS)
        copy = remote(
            outgoing.at[there, used], incoming.at[blk, used], a_send.at[i], a_recv.at[i], samp, there
        )
        copy.start()
        pending.append(copy)
        exchange.append(copy)
    incoming[blk] = outgoing[blk]
    for copy in exchange:
        copy.wait_recv()

    for b in range(TRAITS):
        columns[b * PENALTIES : (b + 1) * PENALTIES, :] = incoming[b, 0:PENALTIES, :]
    columns[STACK:, :] = jnp.broadcast_to(scaled, (SUMS - STACK, rows))
    level = columns[0:STACK, :]
    fold = f_ref[...]
    for k in range(FOLDS):
        weights[k * STACK : (k + 1) * STACK, :] = level * jnp.where(fold == k, mine, 0.0)
    end = FOLDS * STACK
    weights[end:, :] = jnp.zeros((weights.shape[0] - end, rows), jnp.float32)
    local = lax.dot_general(
        columns[...], weights[...], nt, precision=PRECISE, preferred_element_type=jnp.float32
    )
    flat = jnp.concatenate([local[:, 0:LANES], local[:, LANES:]], axis=0)
    for q in range(XS):
        part[q] = flat[q * PARTS : (q + 1) * PARTS]

    sums = []
    for i in range(XS - 1):
        there = lax.rem(x + i + 1, XS)
        sums.append(to_x(there, part.at[there], x_in.at[i], ps.at[i], pr.at[i]))
        sums[i].start()
    for copy in sums:
        copy.wait_recv()
    z_all[z] = part[x] + (x_in[0] + (x_in[1] + x_in[2]))
    spread = {}
    for n, d in enumerate(NEAR):
        spread[-d] = to_z(d, z_all.at[z], z_all.at[z], ds.at[n], dr.at[n])
        spread[-d].start()
    up, down = z_of(-4), z_of(4)
    for e in range(4, 0, -1):
        spread[-4 - e] = to_z(e, z_all.at[up], z_all.at[up], ks_p.at[e - 1], kr_p.at[e - 1])
    for e in range(3, 0, -1):
        spread[4 + e] = to_z(-e, z_all.at[down], z_all.at[down], ks_n.at[e - 1], kr_n.at[e - 1])
    spread[-4].wait_recv()
    for e in range(4, 0, -1):
        spread[-4 - e].start()
    spread[4].wait_recv()
    for e in range(3, 0, -1):
        spread[4 + e].start()
    for o, copy in spread.items():
        if o not in (4, -4):
            copy.wait_recv()
    value = z_all[0]
    for i in range(1, ZS):
        value = value + z_all[i]
    final[x] = value * (FOLDS / samples)
    collect = []
    for i in range(XS - 1):
        there = lax.rem(x + i + 1, XS)
        collect.append(to_x(there, final.at[x], final.at[x], cs.at[i], cr.at[i]))
        collect[i].start()
    for copy in collect:
        copy.wait_recv()
    low = jnp.concatenate([final[0], final[1]], axis=0)
    high = jnp.concatenate([final[2], final[3]], axis=0)
    both = jnp.concatenate([low, high], axis=1)
    for k in range(FOLDS):
        gram_ref[k] = both[0:STACK, k * STACK : (k + 1) * STACK]
        cross_ref[k : k + 1, :] = both[STACK : STACK + 1, k * STACK : (k + 1) * STACK]

    for copy in pending:
        copy.wait_send()

    for n, solver in enumerate(solvers):

        @pl.when(samp != solver)
        def _():
            report(n).wait_send()

    @pl.when(solving)
    def _():
        lax.fori_loop(1, group, wait_give, 0)


def body(genotypes, traits, observed, fold_index):
    rows, local_cols = genotypes.shape
    samples = rows * lax.axis_size("samp")
    markers = local_cols * lax.axis_size("blk")
    vmem = pl.BlockSpec(memory_space=pltpu.VMEM)
    hbm = pl.BlockSpec(memory_space=pltpu.MemorySpace.HBM)
    dma = pltpu.SemaphoreType.DMA
    f32 = jnp.float32
    chunks = (ZS, CHUNK, LANES)
    grams, cross = pl.pallas_call(
        functools.partial(kernel, samples, markers),
        out_shape=(
            jax.ShapeDtypeStruct((FOLDS, STACK, STACK), f32),
            jax.ShapeDtypeStruct((FOLDS, STACK), f32),
        ),
        in_specs=[hbm] * 4,
        out_specs=(vmem, vmem),
        scratch_shapes=[
            pltpu.VMEM((BLOCK, rows), jnp.bfloat16),
            pltpu.VMEM((TRAITS, rows), f32),
            pltpu.VMEM((TRAITS, rows), jnp.int32),
            pltpu.VMEM((1, rows), jnp.int32),
            pltpu.VMEM((LANES, rows), jnp.bfloat16),
            pltpu.VMEM((XS, LAYERS, LANES), f32),
            pltpu.VMEM(chunks, f32),
            pltpu.VMEM(chunks, f32),
            pltpu.VMEM(chunks, f32),
            pltpu.VMEM(chunks, f32),
            pltpu.VMEM((4, CHUNK, LANES), f32),
            pltpu.VMEM((3, CHUNK, LANES), f32),
            pltpu.VMEM((8, CHUNK, LANES), f32),
            pltpu.VMEM((XS, LAYERS, LANES), f32),
            pltpu.VMEM((len(PAIRS), LANES, LANES), f32),
            pltpu.VMEM((len(PAIRS), LANES, LANES), f32),
            pltpu.VMEM((TILES, LANES, LANES), f32),
            pltpu.VMEM((8, WIDTH), f32),
            pltpu.VMEM((PENALTIES, 8, WIDTH), f32),
            pltpu.VMEM((TRAITS, 8, WIDTH), f32),
            pltpu.VMEM((TRAITS, 8, rows), f32),
            pltpu.VMEM((TRAITS, 8, rows), f32),
            pltpu.VMEM((SUMS, rows), f32),
            pltpu.VMEM((2 * LANES, rows), f32),
            pltpu.VMEM((XS, PARTS, LANES), f32),
            pltpu.VMEM((XS - 1, PARTS, LANES), f32),
            pltpu.VMEM((ZS, PARTS, LANES), f32),
            pltpu.VMEM((XS, PARTS, LANES), f32),
            dma((4,)),
            *[dma((ZS,)) for _ in range(6)],
            *[dma((4,)) for _ in range(2)],
            *[dma((3,)) for _ in range(2)],
            *[dma((8,)) for _ in range(2)],
            dma((ZS // REACH * PENALTIES,)),
            dma((ZS * XS,)),
            dma((REACH * XS,)),
            dma((PENALTIES,)),
            *[dma((TRAITS - 1,)) for _ in range(2)],
            *[dma((XS - 1,)) for _ in range(2)],
            *[dma((8,)) for _ in range(2)],
            *[dma((4,)) for _ in range(2)],
            *[dma((3,)) for _ in range(2)],
            *[dma((XS - 1,)) for _ in range(2)],
        ],
        compiler_params=pltpu.CompilerParams(
            collective_id=0, has_side_effects=True, vmem_limit_bytes=67043328
        ),
        name="ridge",
    )(genotypes.T, traits.T, observed.T, fold_index.reshape(1, rows))
    return grams[None], cross[None]


def solution(mesh):
    in_specs = (P("samp", "blk"), P("samp", None), P("samp", None), P("samp"))
    out_specs = (P("blk", None, None, None), P("blk", None, None))
    return jax.shard_map(body, mesh=mesh, in_specs=in_specs, out_specs=out_specs, check_vma=False)
```

```python
import functools

import jax
import jax.numpy as jnp
from jax import lax
from jax.experimental import pallas as pl
from jax.experimental.pallas import tpu as pltpu
from jax.sharding import PartitionSpec as P

BLOCK = 500
TRAITS = 8
FOLDS = 5
HERITABILITY = (0.01, 0.25, 0.5, 0.75, 0.99)
PENALTIES = len(HERITABILITY)
PRECISE = lax.Precision.HIGHEST
MESH = pl.DeviceIdType.MESH

XS = 4
LANES = 128
TILES = 4
WIDTH = TILES * LANES
ONES = BLOCK
PAIRS = [(i, j) for i in range(TILES) for j in range(i, TILES)]
EXTRA = 24
FLAT = len(PAIRS) * LANES + TILES * EXTRA
QUARTER = FLAT // XS
ZS = 16
CHUNK = 24
LAYERS = ZS * CHUNK
STACK = PENALTIES * 8
SUMS = 48
PARTS = 2 * SUMS // XS
ORDER = [8, 7, 6, 5, -7, -6, -5, -4, 4, 3, 2, 1, -3, -2, -1, 0]
NEAR = [4, -4, 3, -3, 2, -2, 1, -1]
REACH = 8
SOLVERS = [(3, 0), (3, 1), (3, 2), (3, 3), (4, 1)]


def pieces(start, rows):
    out = []
    while rows > 0:
        quarter, row = divmod(start, QUARTER)
        take = min(rows, QUARTER - row)
        out.append((quarter, row, take))
        start += take
        rows -= take
    return out


def put(ref, start, value):
    done = 0
    for quarter, row, take in pieces(start, value.shape[0]):
        ref[quarter, row : row + take, :] = value[done : done + take]
        done += take


def get(ref, start, rows):
    parts = [ref[quarter, row : row + take, :] for quarter, row, take in pieces(start, rows)]
    return parts[0] if len(parts) == 1 else jnp.concatenate(parts, axis=0)


def split3(value):
    first = value.astype(jnp.bfloat16).astype(jnp.float32)
    rest = value - first
    second = rest.astype(jnp.bfloat16).astype(jnp.float32)
    third = rest - second
    return first, second, third


def remote(src, dst, send, recv, samp, blk):
    return pltpu.make_async_remote_copy(
        src_ref=src,
        dst_ref=dst,
        send_sem=send,
        recv_sem=recv,
        device_id=(samp, blk),
        device_id_type=MESH,
    )


def invert(a_ref):
    lane = lax.broadcasted_iota(jnp.int32, (8, LANES), 1)
    sub = lax.broadcasted_iota(jnp.int32, (8, LANES), 0)
    wide = lax.broadcasted_iota(jnp.int32, (LANES, LANES), 1)

    def columns_of(strip, base):
        return [jnp.broadcast_to(strip[:, base + j : base + j + 1], (8, LANES)) for j in range(8)]

    def advance(strip, base, solved):
        cols = columns_of(strip, base)
        terms = [cols[j] * solved[j : j + 1, :] for j in range(8)]
        while len(terms) > 1:
            terms = [terms[i] + terms[i + 1] for i in range(0, len(terms), 2)]
        inside = jnp.logical_and(lane >= base, lane < base + 8)
        return jnp.where(inside, 0.0, strip) - terms[0]

    def pivots(strip, base):
        cols = columns_of(strip, base)
        inside = jnp.logical_and(lane >= base, lane < base + 8)
        solved = jnp.where(inside, jnp.where(lane - base == sub, -1.0, 0.0), strip)
        for j in range(0, 8, 2):
            one, two = cols[j], cols[j + 1]
            a, b = one[j : j + 1, :], two[j : j + 1, :]
            c, d = one[j + 1 : j + 2, :], two[j + 1 : j + 2, :]
            inverse = 1.0 / (a * d - b * c)
            a, b, c, d = d * inverse, b * inverse, c * inverse, a * inverse

            def step(value):
                top, low = value[j : j + 1, :], value[j + 1 : j + 2, :]
                top, low = a * top - b * low, d * low - c * top
                rest = value - one * top - two * low
                return jnp.where(sub == j, top, jnp.where(sub == j + 1, low, rest))

            solved = step(solved)
            for m in range(j + 2, 8):
                cols[m] = step(cols[m])
        return solved

    def update(base, strip, solved):
        a1, a2, a3 = split3(strip)
        b1, b2, b3 = split3(solved)
        lhs = jnp.concatenate([a1, a1, a2, a1, a3, a2], axis=0).astype(jnp.bfloat16)
        rhs = jnp.concatenate([b1, b2, b1, b3, b1, b2], axis=0).astype(jnp.bfloat16)
        product = lax.dot_general(
            lhs, rhs, (((0,), (0,)), ((), ())), preferred_element_type=jnp.float32
        )
        within = jnp.logical_and(wide >= base, wide < base + 8)
        a_ref[...] = jnp.where(within, 0.0, a_ref[...]) - product
        a_ref[base : base + 8, :] = solved

    strip = a_ref[0:8, :]
    before = done = None
    for base in range(0, LANES, 8):
        ahead = (base + 8) % LANES
        coming = a_ref[ahead : ahead + 8, :]
        if base > 0:
            coming = advance(coming, base - 8, done)
        solved = pivots(strip, base)
        if base > 0:
            update(base - 8, before, done)
        before, done = strip, solved
        strip = advance(coming, base, solved)
    update(LANES - 8, before, done)


def solve_local(samples, markers, place, total_ref, beta_ref, cov, work, inv):
    weight = jnp.float32(0.0)
    for r, fraction in enumerate(HERITABILITY):
        value = jnp.float32(markers * (1.0 - fraction) / fraction)
        chosen = place == r if r < PENALTIES - 1 else place >= r
        weight = jnp.where(chosen, value, weight)

    dot = functools.partial(jnp.dot, precision=PRECISE, preferred_element_type=jnp.float32)

    def dot_t(a, b):
        return lax.dot_general(
            a, b, (((0,), (0,)), ((), ())), precision=PRECISE, preferred_element_type=jnp.float32
        )

    def dot_nt(a, b):
        return lax.dot_general(
            a, b, (((1,), (1,)), ((), ())), precision=PRECISE, preferred_element_type=jnp.float32
        )

    slot = {pair: n for n, pair in enumerate(PAIRS)}
    gram = {pair: get(total_ref, n * LANES, LANES) for pair, n in slot.items()}
    extra = [get(total_ref, len(PAIRS) * LANES + j * EXTRA, EXTRA) for j in range(TILES)]
    eye = lax.broadcasted_iota(jnp.int32, (LANES, LANES), 0) == lax.broadcasted_iota(
        jnp.int32, (LANES, LANES), 1
    )
    mark = ONES - (TILES - 1) * LANES
    sums = extra[-1][0:8, mark : mark + 1]
    counts = extra[-1][8:16, mark : mark + 1]
    squares = extra[-1][16:24, mark + 1 : mark + 2]
    mean_trait = sums / counts
    trait_scale = jnp.sqrt(squares / counts - mean_trait * mean_trait + 1e-05)
    lane8 = lax.broadcasted_iota(jnp.int32, (8, LANES), 1)

    sum_row, mean_row, inverse_row, mean_col, inverse_col = [], [], [], [], []
    for j in range(TILES):
        diagonal = jnp.where(eye, gram[(j, j)], 0.0)
        row = extra[j][16:17, :]
        if j == TILES - 1:
            row = jnp.where(lane8[0:1] < mark, row, 0.0)
        col = gram[(j, TILES - 1)][:, mark : mark + 1]
        mean = row / samples
        mean_c = col / samples
        sum_row.append(row)
        mean_row.append(mean)
        mean_col.append(mean_c)
        squares_row = jnp.sum(diagonal, axis=0, keepdims=True)
        squares_col = jnp.sum(diagonal, axis=1, keepdims=True)
        inverse_row.append(1.0 / jnp.sqrt(squares_row / samples - mean * mean + 1e-05))
        inverse_col.append(1.0 / jnp.sqrt(squares_col / samples - mean_c * mean_c + 1e-05))
    lane = lax.broadcasted_iota(jnp.int32, (LANES, LANES), 1)
    sub = lax.broadcasted_iota(jnp.int32, (LANES, LANES), 0)
    for (i, j), n in slot.items():
        value = (gram[(i, j)] - mean_col[i] * sum_row[j]) * inverse_col[i] * inverse_row[j]
        if j == TILES - 1:
            value = jnp.where(lane < mark, value, 0.0)
        if i == TILES - 1:
            value = jnp.where(sub < mark, value, 0.0)
        cov[n] = value
        work[n] = jnp.where(eye, value + weight, value) if i == j else value
    side = []
    for j in range(TILES):
        value = (extra[j][0:8] - extra[j][8:16] * mean_trait) / trait_scale * inverse_row[j]
        if j == TILES - 1:
            value = jnp.where(lane8 < mark, value, 0.0)
        side.append(value)

    for k in range(TILES):
        a_ref = inv.at[k]
        a_ref[...] = work[slot[(k, k)]]
        invert(a_ref)
        minus = inv[k]
        for j in range(k + 1, TILES):
            ahead = dot(minus, work[slot[(k, j)]])
            for i in range(k + 1, j + 1):
                n = slot[(i, j)]
                work[n] = work[n] + dot_t(work[slot[(k, i)]], ahead)
        if k < TILES - 1:
            part = dot(side[k], minus)
            for j in range(k + 1, TILES):
                side[j] = side[j] + dot(part, work[slot[(k, j)]])

    found = [None] * TILES
    for k in range(TILES - 1, -1, -1):
        value = side[k]
        for j in range(k + 1, TILES):
            value = value - dot_nt(found[j], work[slot[(k, j)]])
        found[k] = -dot(value, inv[k])

    energy = jnp.zeros((8, 1), jnp.float32)
    shift = jnp.zeros((8, 1), jnp.float32)
    betas = []
    for k in range(TILES):
        image = dot(found[k], cov[slot[(k, k)]])
        for j in range(k + 1, TILES):
            image = image + 2.0 * dot_nt(found[j], cov[slot[(k, j)]])
        energy = energy + jnp.sum(image * found[k], axis=1, keepdims=True)
        beta = found[k] * inverse_row[k]
        shift = shift + jnp.sum(beta * mean_row[k], axis=1, keepdims=True)
        betas.append(beta)
    norm = 1.0 / jnp.sqrt(energy / samples + 1e-06)
    for k in range(TILES):
        value = betas[k]
        if k == TILES - 1:
            value = jnp.where(lane8 == mark, -shift, jnp.where(lane8 < mark, value, 0.0))
        value = value * norm
        if k == TILES - 1:
            value = jnp.where(lane8 == mark + 1, mean_trait, value)
            value = jnp.where(lane8 == mark + 2, trait_scale, value)
        beta_ref[:, k * LANES : (k + 1) * LANES] = value


def kernel(
    samples, markers, g_hbm, t_hbm, o_hbm, f_hbm, gram_ref, cross_ref,
    g_ref, t_ref, o_ref, f_ref, last, pay, far_in, fin_l, fin_r, acc, zfar_p, zfar_n, near_in, total,
    cov, work, inv, beta_ref, held, betas, outgoing, incoming, columns, weights, part, x_in,
    z_all, final, in_sem, fs, fr, ls, lr, rs, rr, zs_p, zr_p, zs_n, zr_n, ns, nr, gs, gr, ss, sr, a_send, a_recv, ps, pr, ds, dr, ks_p, kr_p,
    ks_n, kr_n, cs, cr,
):
    samp = lax.axis_index("samp")
    blk = lax.axis_index("blk")
    z = samp // XS
    x = lax.rem(samp, XS)
    right = lax.rem(x + 1, XS)
    left = lax.rem(x + XS - 1, XS)
    far = lax.rem(x + 2, XS)
    pending = []
    group = REACH * XS
    place = lax.rem(samp, group)
    leader = samp - place
    spots = [zo * XS + xo for zo, xo in SOLVERS]
    solvers = [base + spot for base in range(0, ZS * XS, group) for spot in spots]
    solving = functools.reduce(jnp.logical_or, [place == spot for spot in spots])
    penalty = functools.reduce(
        lambda found, r: jnp.where(place == spots[r], r, found), range(PENALTIES), 0
    )

    def z_of(d):
        return lax.rem(z + d + ZS, ZS)

    def rows_of(d):
        return pl.ds(pl.multiple_of(z_of(d) * CHUNK, 8), CHUNK)

    def to_z(d, src, dst, send, recv):
        copy = remote(src, dst, send, recv, z_of(d) * XS + x, blk)
        pending.append(copy)
        return copy

    def to_x(there, src, dst, send, recv):
        copy = remote(src, dst, send, recv, z * XS + there, blk)
        pending.append(copy)
        return copy

    loads = [
        pltpu.make_async_copy(src, dst, in_sem.at[i])
        for i, (src, dst) in enumerate(
            [(t_hbm, t_ref), (o_hbm, o_ref), (f_hbm, f_ref), (g_hbm, g_ref)]
        )
    ]
    for load in loads:
        load.start()

    barrier = pltpu.get_barrier_semaphore()
    x_peers = [z * XS + lax.rem(x + i, XS) for i in range(1, XS)]
    z_peers = [z_of(d) * XS + x for d in NEAR]
    greeted = x_peers + z_peers
    for other in greeted:
        pl.semaphore_signal(barrier, inc=1, device_id=(other, blk), device_id_type=MESH)
    for i in range(1, TRAITS):
        there = lax.rem(blk + i, TRAITS)
        pl.semaphore_signal(barrier, inc=1, device_id=(samp, there), device_id_type=MESH)

    for load in loads:
        load.wait()
    rows = g_ref.shape[1]
    whole = BLOCK // 16 * 16
    start = (TILES - 1) * LANES
    last[0 : whole - start, :] = g_ref[start:whole, :]
    edge = g_ref[whole:BLOCK, :].astype(jnp.float32)
    sub = lax.broadcasted_iota(jnp.int32, (WIDTH - BLOCK, rows), 0)
    edge = jnp.concatenate([edge, (sub == 0).astype(jnp.float32)], axis=0)
    last[whole - start :, :] = edge.astype(jnp.bfloat16)

    def tile(i):
        return last[...] if i == TILES - 1 else g_ref[i * LANES : (i + 1) * LANES, :]

    nt = (((1,), (1,)), ((), ()))
    traits = t_ref[...]
    present = o_ref[...].astype(jnp.float32)
    masked = traits * present
    squares = jnp.sum(masked * traits, axis=1, keepdims=True)
    ones = (lax.broadcasted_iota(jnp.int32, masked.shape, 0) == 0).astype(jnp.float32)
    stacked = jnp.concatenate([*split3(masked), present, ones], axis=0).astype(jnp.bfloat16)
    slot = 0
    for i in range(TILES):
        for j in range(i, TILES):
            value = lax.dot_general(tile(i), tile(j), nt, preferred_element_type=jnp.float32)
            put(pay, slot * LANES, value)
            slot += 1
    for j in range(TILES):
        cols = lax.dot_general(stacked, tile(j), nt, preferred_element_type=jnp.float32)
        rest = cols[32:40]
        if j == TILES - 1:
            lane = lax.broadcasted_iota(jnp.int32, rest.shape, 1)
            rest = jnp.where(lane == ONES + 1 - j * LANES, squares, rest)
        base = len(PAIRS) * LANES + j * EXTRA
        put(pay, base, cols[0:8] + (cols[8:16] + cols[16:24]))
        put(pay, base + 8, cols[24:32])
        put(pay, base + 16, rest)
    for q in range(XS):
        pay[q, QUARTER:, :] = jnp.zeros((LAYERS - QUARTER, LANES), jnp.float32)

    pl.semaphore_wait(barrier, len(greeted) + TRAITS - 1)

    hop, final_l, final_r = [], [], []
    for i, d in enumerate(ORDER):
        here = rows_of(d)
        even_step = i % 2 == 0
        toward, away = (right, left) if even_step else (left, right)
        hop.append(to_x(toward, pay.at[far, here], far_in.at[i], fs.at[i], fr.at[i]))
        goes_r = to_x(right, pay.at[right, here], fin_l.at[i], ls.at[i], lr.at[i])
        goes_l = to_x(left, pay.at[left, here], fin_r.at[i], rs.at[i], rr.at[i])
        final_l.append(goes_r)
        final_r.append(goes_l)

    def first_step(seg):
        for i in range(4 * seg, 4 * seg + 4):
            hop[i].start()
        for i in range(4 * seg, 4 * seg + 4):
            (final_r if i % 2 == 0 else final_l)[i].start()

    def second_step(seg):
        for i in range(4 * seg, 4 * seg + 4):
            here = rows_of(ORDER[i])
            there = right if i % 2 == 0 else left
            hop[i].wait_recv()
            pay[there, here, :] = pay[there, here, :] + far_in[i]
            (final_l if i % 2 == 0 else final_r)[i].start()

    zfar, near = {}, {}
    for i, d in enumerate(ORDER):
        if d > 4:
            zfar[d] = to_z(4, acc.at[i], zfar_p.at[d - 5], zs_p.at[d - 5], zr_p.at[d - 5])
        elif d < -4:
            zfar[d] = to_z(-4, acc.at[i], zfar_n.at[-d - 5], zs_n.at[-d - 5], zr_n.at[-d - 5])
        elif d != 0:
            n = NEAR.index(d)
            near[d] = to_z(d, acc.at[i], near_in.at[n], ns.at[n], nr.at[n])

    def third_step(seg):
        for i in range(4 * seg, 4 * seg + 4):
            d = ORDER[i]
            final_l[i].wait_recv()
            final_r[i].wait_recv()
            value = pay[x, rows_of(d), :] + (fin_l[i] + fin_r[i])
            if 1 <= d <= 4:
                zfar[d + 4].wait_recv()
                value = value + zfar_p[d - 1]
            elif -3 <= d <= -1:
                zfar[d - 4].wait_recv()
                value = value + zfar_n[-d - 1]
            acc[i] = value
            if d in zfar:
                zfar[d].start()
            elif d != 0:
                near[d].start()

    first_step(0)
    first_step(1)
    second_step(0)
    first_step(2)
    second_step(1)
    first_step(3)
    third_step(0)
    second_step(2)
    third_step(1)
    second_step(3)
    third_step(2)
    third_step(3)
    value = acc[ORDER.index(0)]
    for n, d in enumerate(NEAR):
        near[d].wait_recv()
        value = value + near_in[n]
    own = rows_of(0)
    total[x, own, :] = value

    def report(n):
        here = total.at[x, own]
        return remote(here, here, gs.at[n], gr.at[samp], solvers[n], blk)

    for n, solver in enumerate(solvers):

        @pl.when(samp != solver)
        def _():
            report(n).start()

    def give(i):
        other = leader + lax.rem(place + i, group)
        return remote(beta_ref, held.at[penalty], ss.at[i], sr.at[penalty], other, blk)

    def start_give(i, carry):
        give(i).start()
        return carry

    def wait_give(i, carry):
        give(i).wait_send()
        return carry

    def hear(i, carry):
        other = lax.rem(samp + i, ZS * XS)
        there = pl.ds(pl.multiple_of(other // XS * CHUNK, 8), CHUNK)
        there = total.at[lax.rem(other, XS), there]
        pltpu.make_async_copy(there, there, gr.at[other]).wait()
        return carry

    @pl.when(solving)
    def _():
        lax.fori_loop(1, ZS * XS, hear, 0)
        solve_local(samples, markers, penalty, total, beta_ref, cov, work, inv)
        lax.fori_loop(1, group, start_give, 0)
        held[penalty] = beta_ref[...]

    for r in range(PENALTIES):

        @pl.when(place != spots[r])
        def _():
            pltpu.make_async_copy(held.at[r], held.at[r], sr.at[r]).wait()

    mark = ONES
    mean = held[0, :, mark + 1 : mark + 2]
    scale = held[0, :, mark + 2 : mark + 3]
    which = lax.broadcasted_iota(jnp.int32, (8, rows), 0) == blk
    mine = jnp.sum(jnp.where(which, present, 0.0), axis=0, keepdims=True)
    scaled = present * (traits - mean) / scale
    scaled = jnp.sum(jnp.where(which, scaled, 0.0), axis=0, keepdims=True)
    betas[...] = jnp.zeros_like(betas)
    for r in range(PENALTIES):
        betas[:, r, :] = held[r]
    n = TRAITS * 8
    beta = betas[...].reshape(n, WIDTH)
    beta = jnp.concatenate(split3(beta), axis=0).astype(jnp.bfloat16)
    predicted = jnp.dot(beta[:, start:], last[...], preferred_element_type=jnp.float32)
    predicted = predicted + jnp.dot(
        beta[:, :start], g_ref[0:start, :], preferred_element_type=jnp.float32
    )
    predicted = predicted[0:n] + (predicted[n : 2 * n] + predicted[2 * n :])
    outgoing[...] = predicted.reshape(TRAITS, 8, rows)

    used = pl.ds(0, PENALTIES)
    exchange = []
    for i in range(TRAITS - 1):
        there = lax.rem(blk + i + 1, TRAITS)
        copy = remote(
            outgoing.at[there, used], incoming.at[blk, used], a_send.at[i], a_recv.at[i], samp, there
        )
        copy.start()
        pending.append(copy)
        exchange.append(copy)
    incoming[blk] = outgoing[blk]
    for copy in exchange:
        copy.wait_recv()

    for b in range(TRAITS):
        columns[b * PENALTIES : (b + 1) * PENALTIES, :] = incoming[b, 0:PENALTIES, :]
    columns[STACK:, :] = jnp.broadcast_to(scaled, (SUMS - STACK, rows))
    level = columns[0:STACK, :]
    fold = f_ref[...]
    for k in range(FOLDS):
        weights[k * STACK : (k + 1) * STACK, :] = level * jnp.where(fold == k, mine, 0.0)
    end = FOLDS * STACK
    weights[end:, :] = jnp.zeros((weights.shape[0] - end, rows), jnp.float32)
    local = lax.dot_general(
        columns[...], weights[...], nt, precision=PRECISE, preferred_element_type=jnp.float32
    )
    flat = jnp.concatenate([local[:, 0:LANES], local[:, LANES:]], axis=0)
    for q in range(XS):
        part[q] = flat[q * PARTS : (q + 1) * PARTS]

    sums = []
    for i in range(XS - 1):
        there = lax.rem(x + i + 1, XS)
        sums.append(to_x(there, part.at[there], x_in.at[i], ps.at[i], pr.at[i]))
        sums[i].start()
    for copy in sums:
        copy.wait_recv()
    z_all[z] = part[x] + (x_in[0] + (x_in[1] + x_in[2]))
    spread = {}
    for n, d in enumerate(NEAR):
        spread[-d] = to_z(d, z_all.at[z], z_all.at[z], ds.at[n], dr.at[n])
        spread[-d].start()
    up, down = z_of(-4), z_of(4)
    for e in range(4, 0, -1):
        spread[-4 - e] = to_z(e, z_all.at[up], z_all.at[up], ks_p.at[e - 1], kr_p.at[e - 1])
    for e in range(3, 0, -1):
        spread[4 + e] = to_z(-e, z_all.at[down], z_all.at[down], ks_n.at[e - 1], kr_n.at[e - 1])
    spread[-4].wait_recv()
    for e in range(4, 0, -1):
        spread[-4 - e].start()
    spread[4].wait_recv()
    for e in range(3, 0, -1):
        spread[4 + e].start()
    for o, copy in spread.items():
        if o not in (4, -4):
            copy.wait_recv()
    value = z_all[0]
    for i in range(1, ZS):
        value = value + z_all[i]
    final[x] = value * (FOLDS / samples)
    collect = []
    for i in range(XS - 1):
        there = lax.rem(x + i + 1, XS)
        collect.append(to_x(there, final.at[x], final.at[x], cs.at[i], cr.at[i]))
        collect[i].start()
    for copy in collect:
        copy.wait_recv()
    low = jnp.concatenate([final[0], final[1]], axis=0)
    high = jnp.concatenate([final[2], final[3]], axis=0)
    both = jnp.concatenate([low, high], axis=1)
    for k in range(FOLDS):
        gram_ref[k] = both[0:STACK, k * STACK : (k + 1) * STACK]
        cross_ref[k : k + 1, :] = both[STACK : STACK + 1, k * STACK : (k + 1) * STACK]

    for copy in pending:
        copy.wait_send()

    for n, solver in enumerate(solvers):

        @pl.when(samp != solver)
        def _():
            report(n).wait_send()

    @pl.when(solving)
    def _():
        lax.fori_loop(1, group, wait_give, 0)


def body(genotypes, traits, observed, fold_index):
    rows, local_cols = genotypes.shape
    samples = rows * lax.axis_size("samp")
    markers = local_cols * lax.axis_size("blk")
    vmem = pl.BlockSpec(memory_space=pltpu.VMEM)
    hbm = pl.BlockSpec(memory_space=pltpu.MemorySpace.HBM)
    dma = pltpu.SemaphoreType.DMA
    f32 = jnp.float32
    chunks = (ZS, CHUNK, LANES)
    grams, cross = pl.pallas_call(
        functools.partial(kernel, samples, markers),
        out_shape=(
            jax.ShapeDtypeStruct((FOLDS, STACK, STACK), f32),
            jax.ShapeDtypeStruct((FOLDS, STACK), f32),
        ),
        in_specs=[hbm] * 4,
        out_specs=(vmem, vmem),
        scratch_shapes=[
            pltpu.VMEM((BLOCK, rows), jnp.bfloat16),
            pltpu.VMEM((TRAITS, rows), f32),
            pltpu.VMEM((TRAITS, rows), jnp.int32),
            pltpu.VMEM((1, rows), jnp.int32),
            pltpu.VMEM((LANES, rows), jnp.bfloat16),
            pltpu.VMEM((XS, LAYERS, LANES), f32),
            pltpu.VMEM(chunks, f32),
            pltpu.VMEM(chunks, f32),
            pltpu.VMEM(chunks, f32),
            pltpu.VMEM(chunks, f32),
            pltpu.VMEM((4, CHUNK, LANES), f32),
            pltpu.VMEM((3, CHUNK, LANES), f32),
            pltpu.VMEM((8, CHUNK, LANES), f32),
            pltpu.VMEM((XS, LAYERS, LANES), f32),
            pltpu.VMEM((len(PAIRS), LANES, LANES), f32),
            pltpu.VMEM((len(PAIRS), LANES, LANES), f32),
            pltpu.VMEM((TILES, LANES, LANES), f32),
            pltpu.VMEM((8, WIDTH), f32),
            pltpu.VMEM((PENALTIES, 8, WIDTH), f32),
            pltpu.VMEM((TRAITS, 8, WIDTH), f32),
            pltpu.VMEM((TRAITS, 8, rows), f32),
            pltpu.VMEM((TRAITS, 8, rows), f32),
            pltpu.VMEM((SUMS, rows), f32),
            pltpu.VMEM((2 * LANES, rows), f32),
            pltpu.VMEM((XS, PARTS, LANES), f32),
            pltpu.VMEM((XS - 1, PARTS, LANES), f32),
            pltpu.VMEM((ZS, PARTS, LANES), f32),
            pltpu.VMEM((XS, PARTS, LANES), f32),
            dma((4,)),
            *[dma((ZS,)) for _ in range(6)],
            *[dma((4,)) for _ in range(2)],
            *[dma((3,)) for _ in range(2)],
            *[dma((8,)) for _ in range(2)],
            dma((ZS // REACH * PENALTIES,)),
            dma((ZS * XS,)),
            dma((REACH * XS,)),
            dma((PENALTIES,)),
            *[dma((TRAITS - 1,)) for _ in range(2)],
            *[dma((XS - 1,)) for _ in range(2)],
            *[dma((8,)) for _ in range(2)],
            *[dma((4,)) for _ in range(2)],
            *[dma((3,)) for _ in range(2)],
            *[dma((XS - 1,)) for _ in range(2)],
        ],
        compiler_params=pltpu.CompilerParams(
            collective_id=0, has_side_effects=True, vmem_limit_bytes=67043328
        ),
        name="ridge",
    )(genotypes.T, traits.T, observed.T, fold_index.reshape(1, rows))
    return grams[None], cross[None]


def solution(mesh):
    in_specs = (P("samp", "blk"), P("samp", None), P("samp", None), P("samp"))
    out_specs = (P("blk", None, None, None), P("blk", None, None))
    return jax.shard_map(body, mesh=mesh, in_specs=in_specs, out_specs=out_specs, check_vma=False)
```
